32 devices in a mesh: group: 2 (over y), frame: 4 (over z), space: 2 (over x), head: 2 (over core).
Axes of the slice: x: 2, y: 2, z: 4, core: 2. Of those that a mesh axis runs over, the one named last changes fastest.
Arguments:
- queries: bfloat16 [8, 8, 48, 3072], P(('group', 'frame'), 'space', None, 'head'), parts along dimension 0, may hold values from -8 to 8
- keys: bfloat16 [8, 8, 48, 3072], P(('group', 'frame'), 'space', None, 'head'), parts along dimension 0, may hold values from -8 to 8
- values: bfloat16 [8, 8, 48, 3072], P(('group', 'frame'), 'space', None, 'head'), parts along dimension 0, may hold values from -6 to 6
- flags: int32 [4, 4], replicated, may hold values from 0 to 1, as said below
- widths: int32 [4], replicated, may hold values from 0 to 8, as said below
Outputs:
- attended: bfloat16 [8, 8, 48, 3072], P(('group', 'frame'), 'space', None, 'head'), parts along dimension 0
The draws below stay inside these ranges and needn't reach their ends.
There are 2 independent parts, one for each index of `group`. The reference program is written for one: setup_inputs(seed, part) draws one part's arguments, and reference() takes and returns one part's arrays. A program takes and returns all parts, laid end to end along the dimension named above; an argument that names none is the same for every part. Nothing has to cross between parts.
Inputs may be any that keep to these rules, and one draw needn't show every extreme that they name: flags[f, g] = 1 wherever |f - g| <= 1, and flags[0, 3] = flags[3, 0] = 0. widths[0] = 8, and widths never rise with the frame distance.
All inputs are finite; a program needn't handle non-finite values.
Results may differ from the reference program's by a relative error of at most 0.006.
Values may be sent and summed in bfloat16 or wider, within the bound.
A program may use at most 128 MiB of HBM per device.

```python
import jax
import jax.numpy as jnp
from jax import lax

HEADS = 24
HEAD_DIM = 128
PC = 48
FRAMES = 4
ROWS = 8


def draw_queries(key, part):
    shape = (FRAMES, ROWS, PC, HEADS, HEAD_DIM)
    base = jax.random.normal(jax.random.fold_in(key, 11), shape, jnp.float32)
    result = jnp.clip(1.5 * base, -8.0, 8.0)
    return result.reshape(FRAMES, ROWS, PC, HEADS * HEAD_DIM).astype(jnp.bfloat16)


def draw_keys(key, part):
    shape = (FRAMES, ROWS, PC, HEADS, HEAD_DIM)
    base = jax.random.normal(jax.random.fold_in(key, 21), shape, jnp.float32)
    result = jnp.clip(base, -6.0, 6.0)
    return result.reshape(FRAMES, ROWS, PC, HEADS * HEAD_DIM).astype(jnp.bfloat16)


def draw_flags(key, part):
    levels = jax.random.randint(jax.random.fold_in(key, 31), (FRAMES, FRAMES), 0, 16)
    frame_ids = jnp.arange(FRAMES, dtype=jnp.int32)
    distance = jnp.abs(frame_ids[:, None] - frame_ids[None, :])
    base_flags = (levels * distance < 24).astype(jnp.int32)
    return jnp.where(distance == FRAMES - 1, 0, base_flags).astype(jnp.int32)


def draw_widths(key, part):
    distance = jnp.arange(FRAMES, dtype=jnp.int32)
    first_band = jax.random.randint(jax.random.fold_in(key, 41), (), 1, 3)
    band_count = jnp.zeros((FRAMES,), jnp.int32)
    for level in range(8):
        band_count = band_count + (distance >= first_band * 2 ** level).astype(jnp.int32)
    extra_drop = jax.random.randint(jax.random.fold_in(key, 42), (FRAMES,), 0, 2)
    extra_drop = jnp.where(distance == 0, 0, extra_drop)
    shifts = jnp.minimum(band_count + extra_drop, 30)
    raw_widths = jnp.right_shift(jnp.full((FRAMES,), ROWS, jnp.int32), shifts)
    return lax.cummin(raw_widths, axis=0).astype(jnp.int32)


def block_scale(stream_key, extent, pieces, least, largest):
    def one(dim, parts):
        heights = jax.random.uniform(jax.random.fold_in(jax.random.fold_in(stream_key, 6), dim), (parts,), jnp.float32, least / len(pieces), largest / len(pieces))
        return jnp.repeat(jnp.exp(heights), extent[dim] // parts).reshape((-1,) + (1,) * (len(extent) - dim - 1))

    factor_of = one(*pieces[0])
    for cut in pieces[1:]:
        factor_of = factor_of * one(*cut)
    return factor_of


def bell_draw(stream_key, dims, spread, reach, split=(), kind=jnp.bfloat16):
    values = jax.random.normal(stream_key, dims, jnp.float32) * spread
    if len(split) > 0:
        values = block_scale(stream_key, dims, split, -0.22, 0.18) * values
    return jnp.clip(values, min=-reach, max=reach).astype(kind)


def setup_inputs(seed: int = 0, part: int = 0) -> dict:
    arg_keys = jax.random.split(jax.random.key(seed), 6)
    part_keys = jax.random.split(jax.random.fold_in(arg_keys[5], part), 6)
    return {
        "queries": draw_queries(jax.random.fold_in(jax.random.fold_in(arg_keys[5], part), 71), part),
        "keys": draw_keys(jax.random.fold_in(jax.random.fold_in(arg_keys[5], part), 71), part),
        "values": bell_draw(part_keys[2], (FRAMES, ROWS, PC, HEADS * HEAD_DIM), 1.0, 6.0, ((0, 4), (1, 2), (3, 2))),
        "flags": draw_flags(jax.random.fold_in(arg_keys[5], 71), part),
        "widths": draw_widths(jax.random.fold_in(arg_keys[5], 71), part),
    }


def reference(queries, keys, values, flags, widths):
    frame_count, row_count, column_count, features = queries.shape
    head_count = features // HEAD_DIM
    per_frame = row_count * column_count
    scale = 1.0 / (HEAD_DIM ** 0.5)
    query_tok = queries.reshape(frame_count, per_frame, head_count, HEAD_DIM)
    key_tok = keys.reshape(frame_count * per_frame, head_count, HEAD_DIM)
    value_tok = values.reshape(frame_count * per_frame, head_count, HEAD_DIM)
    token_ids = jnp.arange(frame_count * per_frame, dtype=jnp.int32)
    key_frame = token_ids // per_frame
    key_row = (token_ids // column_count) % row_count
    query_row = jnp.arange(per_frame, dtype=jnp.int32) // column_count

    def frame_out(query_frame):
        frame_query = lax.dynamic_index_in_dim(query_tok, query_frame, 0, False)
        flag_row = lax.dynamic_index_in_dim(flags, query_frame, 0, False)
        reach_rows = widths[jnp.abs(query_frame - key_frame)]
        allowed = (flag_row[key_frame] > 0)[None, :] & (
            jnp.abs(query_row[:, None] - key_row[None, :]) <= reach_rows[None, :])

        def head_out(head):
            head_query = lax.dynamic_index_in_dim(frame_query, head, 1, False)
            head_key = lax.dynamic_index_in_dim(key_tok, head, 1, False)
            head_value = lax.dynamic_index_in_dim(value_tok, head, 1, False)
            scores = jnp.dot(head_query, head_key.T, preferred_element_type=jnp.float32) * scale
            scores = jnp.where(allowed, scores, -jnp.inf)
            top = jnp.max(scores, axis=1, keepdims=True)
            weights = jnp.where(allowed, jnp.exp(scores - top), 0.0)
            total = jnp.sum(weights, axis=1, keepdims=True)
            blended = jnp.dot(weights.astype(jnp.bfloat16), head_value, preferred_element_type=jnp.float32)
            return blended / total

        outputs = lax.map(head_out, jnp.arange(head_count, dtype=jnp.int32))
        return jnp.transpose(outputs, (1, 0, 2)).reshape(per_frame, features)

    result = lax.map(frame_out, jnp.arange(frame_count, dtype=jnp.int32))
    return result.reshape(queries.shape).astype(jnp.bfloat16)
```

```python
import functools
import math

import jax
import jax.numpy as jnp
from jax import lax
from jax.experimental import pallas as pl
from jax.experimental.pallas import tpu as pltpu
from jax.sharding import PartitionSpec as P

HEAD_DIM = 128
NEG_FILL = -1e30
SCALE = math.log2(math.e) / HEAD_DIM**0.5
MESH = pl.DeviceIdType.MESH
LEFT, RIGHT = 0, 1


def kernel(
    frames,
    parts,
    heads,
    columns,
    q_ref,
    k_ref,
    v_ref,
    flags_in,
    widths_in,
    out_ref,
    kv,
    qb,
    ob,
    dist,
    wb,
    top,
    total,
    acc,
    local_sem,
    x_send,
    x_recv,
    z_send,
    z_recv,
    f_send,
    f_recv,
    o_send,
    o_recv,
    flags_ref,
    widths_ref,
    table_sem,
):
    frame = lax.axis_index("frame")
    part = lax.axis_index("space")
    rows = q_ref.shape[0]
    tokens = parts * rows
    width = heads * HEAD_DIM
    far = frames - 2
    inputs = (k_ref, v_ref, q_ref)

    def lane(head):
        return pl.ds(pl.multiple_of(head * HEAD_DIM, HEAD_DIM), HEAD_DIM)

    def span(p):
        return pl.ds(pl.multiple_of(p * width, HEAD_DIM), width)

    def peer(j):
        return lax.rem(part + j, parts)

    def home(i):
        return qb.at[part] if i == 2 else kv.at[frame, i, part]

    barrier = pltpu.get_barrier_semaphore()
    for j in range(1, parts):
        pl.semaphore_signal(barrier, inc=1, device_id={"space": peer(j)}, device_id_type=MESH)

    @pl.when(frame > 0)
    def _():
        pl.semaphore_signal(barrier, inc=1, device_id={"frame": frame - 1}, device_id_type=MESH)

    @pl.when(frame < frames - 1)
    def _():
        pl.semaphore_signal(barrier, inc=1, device_id={"frame": frame + 1}, device_id_type=MESH)

    def local_copy(i):
        return pltpu.make_async_copy(inputs[i].at[:, span(part)], home(i), local_sem.at[i])

    def exchange(j, i):
        return pltpu.make_async_remote_copy(
            src_ref=inputs[i].at[:, span(peer(j))],
            dst_ref=home(i),
            send_sem=x_send.at[i, j - 1],
            recv_sem=x_recv.at[i, j - 1],
            device_id={"space": peer(j)},
            device_id_type=MESH,
        )

    def o_exchange(h, j):
        return pltpu.make_async_remote_copy(
            src_ref=ob.at[peer(j), :, lane(h)],
            dst_ref=out_ref.at[:, lane(part * heads + h)],
            send_sem=o_send.at[j - 1, h],
            recv_sem=o_recv.at[j - 1, h],
            device_id={"space": peer(j)},
            device_id_type=MESH,
        )

    def towards(side):
        return 1 if side == RIGHT else -1

    def hop(side, step, i, p, src=None, back=False):
        ahead = towards(side)
        owner = frame - ahead * (step if back else step - 1)
        block = kv.at[owner, i, p]
        return pltpu.make_async_remote_copy(
            src_ref=block if src is None else src,
            dst_ref=block,
            send_sem=z_send.at[side, step - 1, i, p],
            recv_sem=z_recv.at[side, step - 1, i, p],
            device_id={"frame": frame - ahead if back else frame + ahead},
            device_id_type=MESH,
        )

    def fine(side, h, back=False):
        ahead = towards(side)
        owner = frame - ahead * (far if back else far - 1)
        block = kv.at[owner, 1, :, :, lane(h)]
        return pltpu.make_async_remote_copy(
            src_ref=block,
            dst_ref=block,
            send_sem=f_send.at[side, h],
            recv_sem=f_recv.at[side, h],
            device_id={"frame": frame - ahead if back else frame + ahead},
            device_id_type=MESH,
        )

    def can_send(side, step):
        if side == RIGHT:
            return (frame < frames - 1) & (frame - (step - 1) >= 0)
        return (frame > 0) & (frame + (step - 1) <= frames - 1)

    def gets(side, step):
        if side == RIGHT:
            return frame - step >= 0
        return frame + step <= frames - 1

    def source(side, step):
        return frame - step if side == RIGHT else frame + step

    def each_head(body):
        @pl.loop(0, heads)
        def _(h):
            body(h)

    pl.semaphore_wait(
        barrier,
        parts - 1 + jnp.where(frame > 0, 1, 0) + jnp.where(frame < frames - 1, 1, 0),
    )

    for i in (0, 1):
        for j in range(1, parts):
            exchange(j, i).start()
        for side in (LEFT, RIGHT):

            @pl.when(can_send(side, 1))
            def _():
                hop(side, 1, i, part, inputs[i].at[:, span(part)]).start()

    tables = (
        pltpu.make_async_copy(flags_in, flags_ref, table_sem.at[0]),
        pltpu.make_async_copy(widths_in, widths_ref, table_sem.at[1]),
    )
    for copy in tables:
        copy.start()
    for i in range(3):
        local_copy(i).start()
    for j in range(1, parts):
        exchange(j, 2).start()

    def row_of(axis):
        at = lax.broadcasted_iota(jnp.int32, (tokens, tokens), axis).astype(jnp.float32)
        return jnp.floor((at + 0.5) * (1.0 / columns))

    dist[...] = jnp.abs(row_of(0) - row_of(1))
    top[...] = jnp.full(top.shape, NEG_FILL, jnp.float32)
    total[...] = jnp.zeros(total.shape, jnp.float32)
    acc[...] = jnp.zeros(acc.shape, jnp.float32)

    def await_piece(side, step, i, p):
        @pl.when(gets(side, step))
        def _():
            hop(side, step, i, p, back=True).wait_recv()

    def relay_piece(side, step, i, p):
        @pl.when(gets(side, step) & can_send(side, step + 1))
        def _():
            hop(side, step + 1, i, p).start()

    def relay_fine(step):
        for side in (LEFT, RIGHT):

            @pl.when(gets(side, step) & can_send(side, step + 1))
            def _():
                each_head(lambda h: fine(side, h).start())

    def pass_piece(i):
        for j in range(1, parts):
            p = lax.rem(part - j + parts, parts)
            exchange(j, i).wait_recv()
            for side in (LEFT, RIGHT):

                @pl.when(can_send(side, 1))
                def _():
                    hop(side, 1, i, p).start()

    def take(step, i, p):
        for side in (LEFT, RIGHT):
            await_piece(side, step, i, p)
            if far > 1:
                relay_piece(side, step, i, p)

    pass_piece(0)
    take(1, 0, part)
    pass_piece(1)
    for copy in tables:
        copy.wait()

    def masked(h, g, p):
        gap = jnp.abs(frame - g)
        reach = jnp.where(flags_ref[frame, g] > 0, widths_ref[gap], -1).astype(jnp.float32)
        cut = pl.ds(p * rows, rows)
        keys = kv[g, 0, :, :, lane(h)].reshape(tokens, HEAD_DIM)
        scores = lax.dot_general(
            qb[p, :, lane(h)], keys, (((1,), (1,)), ((), ())), preferred_element_type=jnp.float32
        )
        scores = jnp.where(dist[cut, :] <= reach, scores, NEG_FILL)
        old_top = top[h, cut]
        new_top = jnp.maximum(old_top, jnp.max(scores, axis=1, keepdims=True))
        weights = jnp.exp2((scores - new_top) * SCALE)
        keep = jnp.exp2((old_top - new_top) * SCALE)
        top[h, cut] = new_top
        total[h, cut] = total[h, cut] * keep + jnp.sum(weights, axis=1, keepdims=True)
        return weights.astype(jnp.bfloat16), keep

    def mixed(weights, h, g):
        vals = kv[g, 1, :, :, lane(h)].reshape(tokens, HEAD_DIM)
        return jnp.dot(weights, vals, preferred_element_type=jnp.float32)

    def update(h, g):
        for p in range(parts):
            cut = pl.ds(p * rows, rows)
            weights, keep = masked(h, g, p)
            acc[h, cut] = acc[h, cut] * keep + mixed(weights, h, g)

    def blend(step):
        def body(h):
            for side in (LEFT, RIGHT):

                @pl.when(gets(side, step))
                def _():
                    update(h, source(side, step))

        each_head(body)

    for j in range(1, parts):
        take(1, 0, peer(j))
    for i in range(3):
        local_copy(i).wait()
    for j in range(1, parts):
        exchange(j, 2).wait_recv()
    each_head(lambda h: update(h, frame))

    def take_values(step):
        for p in range(parts):
            for side in (LEFT, RIGHT):
                await_piece(side, step, 1, p)
                if far > 2:

                    @pl.when(step + 1 < far)
                    def _():
                        relay_piece(side, step, 1, p)

        if far > 1:
            if far == 2:
                relay_fine(step)
            else:

                @pl.when(step + 1 == far)
                def _():
                    relay_fine(step)

    take_values(1)
    blend(1)

    if far > 2:

        @pl.loop(2, far)
        def _(step):
            for p in range(parts):
                take(step, 0, p)
            take_values(step)
            blend(step)

    if far > 1:
        for p in range(parts):
            for side in (LEFT, RIGHT):
                await_piece(side, far, 0, p)

    def last(h):
        if far > 1:
            for side in (LEFT, RIGHT):

                @pl.when(gets(side, far))
                def _():
                    for p in range(parts):
                        cut = pl.ds(p * rows, rows)
                        weights, keep = masked(h, source(side, far), p)
                        wb[side, cut] = weights
                        acc[h, cut] = acc[h, cut] * keep

        total[h] = 1.0 / total[h]
        if far > 1:
            for side in (LEFT, RIGHT):

                @pl.when(gets(side, far))
                def _():
                    fine(side, h, back=True).wait_recv()

        def finish(p):
            cut = pl.ds(pl.multiple_of(p * rows, rows), rows)
            if far > 1:
                for side in (LEFT, RIGHT):

                    @pl.when(gets(side, far))
                    def _():
                        acc[h, cut] = acc[h, cut] + mixed(wb[side, cut], h, source(side, far))

            return (acc[h, cut] * total[h, cut]).astype(jnp.bfloat16)

        for j in range(1, parts):
            ob[peer(j), :, lane(h)] = finish(peer(j))
            o_exchange(h, j).start()
        out_ref[:, lane(part * heads + h)] = finish(part)

    each_head(last)

    def close_head(h):
        for j in range(1, parts):
            o_exchange(h, j).wait()
        if far > 1:
            for side in (LEFT, RIGHT):

                @pl.when(can_send(side, far))
                def _():
                    fine(side, h).wait_send()

    for i in range(3):
        for j in range(1, parts):
            exchange(j, i).wait_send()

    @pl.loop(1, far + 1)
    def _(step):
        for side in (LEFT, RIGHT):

            @pl.when(can_send(side, step))
            def _():
                for p in range(parts):
                    hop(side, step, 0, p).wait_send()

                    @pl.when((step < far) | (step == 1))
                    def _():
                        hop(side, step, 1, p).wait_send()

    each_head(close_head)


def shards(frames, parts, queries, keys, values, flags, widths):
    shape = queries.shape
    columns, features = shape[2], shape[3]
    rows = shape[1] * columns
    heads = features // HEAD_DIM // parts
    tokens = rows * parts
    far = frames - 2
    flat = [a.reshape(rows, features) for a in (queries, keys, values)]
    any_spec = pl.BlockSpec(memory_space=pl.ANY)
    others = max(parts - 1, 1)
    dma = pltpu.SemaphoreType.DMA
    out = pl.pallas_call(
        functools.partial(kernel, frames, parts, heads, columns),
        out_shape=pltpu.VMEM((rows, features), jnp.bfloat16),
        in_specs=[any_spec] * 5,
        out_specs=pl.BlockSpec(memory_space=pltpu.VMEM),
        scratch_shapes=[
            pltpu.VMEM((frames, 2, parts, rows, heads * HEAD_DIM), jnp.bfloat16),
            pltpu.VMEM((parts, rows, heads * HEAD_DIM), jnp.bfloat16),
            pltpu.VMEM((parts, rows, heads * HEAD_DIM), jnp.bfloat16),
            pltpu.VMEM((tokens, tokens), jnp.float32),
            pltpu.VMEM((2, tokens, tokens), jnp.bfloat16),
            pltpu.VMEM((heads, tokens, 1), jnp.float32),
            pltpu.VMEM((heads, tokens, 1), jnp.float32),
            pltpu.VMEM((heads, tokens, HEAD_DIM), jnp.float32),
            dma((3,)),
            dma((3, others)),
            dma((3, others)),
            dma((2, far, 2, parts)),
            dma((2, far, 2, parts)),
            dma((2, heads)),
            dma((2, heads)),
            dma((others, heads)),
            dma((others, heads)),
            pltpu.SMEM(flags.shape, jnp.int32),
            pltpu.SMEM(widths.shape, jnp.int32),
            dma((2,)),
        ],
        compiler_params=pltpu.CompilerParams(collective_id=0, has_side_effects=True),
    )(*flat, flags, widths)
    return out.reshape(shape)


def solution(mesh):
    spec = P(("group", "frame"), "space", None, "head")
    return jax.shard_map(
        functools.partial(shards, mesh.shape["frame"], mesh.shape["space"]),
        mesh=mesh,
        in_specs=(spec, spec, spec, P(), P()),
        out_specs=spec,
        check_vma=False,
    )
```

```python
import functools
import math

import jax
import jax.numpy as jnp
from jax import lax
from jax.experimental import pallas as pl
from jax.experimental.pallas import tpu as pltpu
from jax.sharding import PartitionSpec as P

HEAD_DIM = 128
NEG_FILL = -1e30
SCALE = math.log2(math.e) / HEAD_DIM**0.5
MESH = pl.DeviceIdType.MESH
LEFT, RIGHT = 0, 1


def kernel(
    frames,
    parts,
    heads,
    columns,
    q_ref,
    k_ref,
    v_ref,
    flags_in,
    widths_in,
    out_ref,
    kv,
    qb,
    ob,
    dist,
    wb,
    top,
    total,
    acc,
    local_sem,
    x_send,
    x_recv,
    z_send,
    z_recv,
    f_send,
    f_recv,
    o_send,
    o_recv,
    flags_ref,
    widths_ref,
    table_sem,
):
    frame = lax.axis_index("frame")
    part = lax.axis_index("space")
    rows = q_ref.shape[0]
    tokens = parts * rows
    width = heads * HEAD_DIM
    far = frames - 2
    inputs = (k_ref, v_ref, q_ref)

    def lane(head):
        return pl.ds(pl.multiple_of(head * HEAD_DIM, HEAD_DIM), HEAD_DIM)

    def span(p):
        return pl.ds(pl.multiple_of(p * width, HEAD_DIM), width)

    def peer(j):
        return lax.rem(part + j, parts)

    def home(i):
        return qb.at[part] if i == 2 else kv.at[frame, i, part]

    barrier = pltpu.get_barrier_semaphore()
    for j in range(1, parts):
        pl.semaphore_signal(barrier, inc=1, device_id={"space": peer(j)}, device_id_type=MESH)

    @pl.when(frame > 0)
    def _():
        pl.semaphore_signal(barrier, inc=1, device_id={"frame": frame - 1}, device_id_type=MESH)

    @pl.when(frame < frames - 1)
    def _():
        pl.semaphore_signal(barrier, inc=1, device_id={"frame": frame + 1}, device_id_type=MESH)

    def local_copy(i):
        return pltpu.make_async_copy(inputs[i].at[:, span(part)], home(i), local_sem.at[i])

    def exchange(j, i):
        return pltpu.make_async_remote_copy(
            src_ref=inputs[i].at[:, span(peer(j))],
            dst_ref=home(i),
            send_sem=x_send.at[i, j - 1],
            recv_sem=x_recv.at[i, j - 1],
            device_id={"space": peer(j)},
            device_id_type=MESH,
        )

    def o_exchange(h, j):
        return pltpu.make_async_remote_copy(
            src_ref=ob.at[peer(j), :, lane(h)],
            dst_ref=out_ref.at[:, lane(part * heads + h)],
            send_sem=o_send.at[j - 1, h],
            recv_sem=o_recv.at[j - 1, h],
            device_id={"space": peer(j)},
            device_id_type=MESH,
        )

    def towards(side):
        return 1 if side == RIGHT else -1

    def hop(side, step, i, p, src=None, back=False):
        ahead = towards(side)
        owner = frame - ahead * (step if back else step - 1)
        block = kv.at[owner, i, p]
        return pltpu.make_async_remote_copy(
            src_ref=block if src is None else src,
            dst_ref=block,
            send_sem=z_send.at[side, step - 1, i, p],
            recv_sem=z_recv.at[side, step - 1, i, p],
            device_id={"frame": frame - ahead if back else frame + ahead},
            device_id_type=MESH,
        )

    def fine(side, h, back=False):
        ahead = towards(side)
        owner = frame - ahead * (far if back else far - 1)
        block = kv.at[owner, 1, :, :, lane(h)]
        return pltpu.make_async_remote_copy(
            src_ref=block,
            dst_ref=block,
            send_sem=f_send.at[side, h],
            recv_sem=f_recv.at[side, h],
            device_id={"frame": frame - ahead if back else frame + ahead},
            device_id_type=MESH,
        )

    def can_send(side, step):
        if side == RIGHT:
            return (frame < frames - 1) & (frame - (step - 1) >= 0)
        return (frame > 0) & (frame + (step - 1) <= frames - 1)

    def gets(side, step):
        if side == RIGHT:
            return frame - step >= 0
        return frame + step <= frames - 1

    def source(side, step):
        return frame - step if side == RIGHT else frame + step

    def each_head(body):
        @pl.loop(0, heads)
        def _(h):
            body(h)

    pl.semaphore_wait(
        barrier,
        parts - 1 + jnp.where(frame > 0, 1, 0) + jnp.where(frame < frames - 1, 1, 0),
    )

    for i in (0, 1):
        for j in range(1, parts):
            exchange(j, i).start()
        for side in (LEFT, RIGHT):

            @pl.when(can_send(side, 1))
            def _():
                hop(side, 1, i, part, inputs[i].at[:, span(part)]).start()

    tables = (
        pltpu.make_async_copy(flags_in, flags_ref, table_sem.at[0]),
        pltpu.make_async_copy(widths_in, widths_ref, table_sem.at[1]),
    )
    for copy in tables:
        copy.start()
    for i in range(3):
        local_copy(i).start()
    for j in range(1, parts):
        exchange(j, 2).start()

    def row_of(axis):
        at = lax.broadcasted_iota(jnp.int32, (tokens, tokens), axis).astype(jnp.float32)
        return jnp.floor((at + 0.5) * (1.0 / columns))

    dist[...] = jnp.abs(row_of(0) - row_of(1))
    top[...] = jnp.full(top.shape, NEG_FILL, jnp.float32)
    total[...] = jnp.zeros(total.shape, jnp.float32)
    acc[...] = jnp.zeros(acc.shape, jnp.float32)

    def await_piece(side, step, i, p):
        @pl.when(gets(side, step))
        def _():
            hop(side, step, i, p, back=True).wait_recv()

    def relay_piece(side, step, i, p):
        @pl.when(gets(side, step) & can_send(side, step + 1))
        def _():
            hop(side, step + 1, i, p).start()

    def relay_fine(step):
        for side in (LEFT, RIGHT):

            @pl.when(gets(side, step) & can_send(side, step + 1))
            def _():
                each_head(lambda h: fine(side, h).start())

    def pass_piece(i):
        for j in range(1, parts):
            p = lax.rem(part - j + parts, parts)
            exchange(j, i).wait_recv()
            for side in (LEFT, RIGHT):

                @pl.when(can_send(side, 1))
                def _():
                    hop(side, 1, i, p).start()

    def take(step, i, p):
        for side in (LEFT, RIGHT):
            await_piece(side, step, i, p)
            if far > 1:
                relay_piece(side, step, i, p)

    pass_piece(0)
    take(1, 0, part)
    pass_piece(1)
    for copy in tables:
        copy.wait()

    def masked(h, g):
        gap = jnp.abs(frame - g)
        reach = jnp.where(flags_ref[frame, g] > 0, widths_ref[gap], -1).astype(jnp.float32)
        keys = kv[g, 0, :, :, lane(h)].reshape(tokens, HEAD_DIM)
        queries = qb[:, :, lane(h)].reshape(tokens, HEAD_DIM)
        scores = lax.dot_general(
            keys, queries, (((1,), (1,)), ((), ())), preferred_element_type=jnp.float32
        )
        scores = jnp.where(dist[...] <= reach, scores, NEG_FILL)
        old_top = top[h]
        new_top = jnp.maximum(old_top, jnp.max(scores, axis=0, keepdims=True))
        weights = jnp.exp2((scores - new_top) * SCALE)
        keep = jnp.exp2((old_top - new_top) * SCALE)
        top[h] = new_top
        total[h] = total[h] * keep + jnp.sum(weights, axis=0, keepdims=True)
        return weights.astype(jnp.bfloat16), keep

    def mixed(weights, h, g):
        vals = kv[g, 1, :, :, lane(h)].reshape(tokens, HEAD_DIM)
        return lax.dot_general(
            vals, weights, (((0,), (0,)), ((), ())), preferred_element_type=jnp.float32
        )

    def update(h, g):
        weights, keep = masked(h, g)
        acc[h] = acc[h] * keep + mixed(weights, h, g)

    def blend(step):
        def body(h):
            for side in (LEFT, RIGHT):

                @pl.when(gets(side, step))
                def _():
                    update(h, source(side, step))

        each_head(body)

    for j in range(1, parts):
        take(1, 0, peer(j))
    for i in range(3):
        local_copy(i).wait()
    for j in range(1, parts):
        exchange(j, 2).wait_recv()
    each_head(lambda h: update(h, frame))

    def take_values(step):
        for p in range(parts):
            for side in (LEFT, RIGHT):
                await_piece(side, step, 1, p)
                if far > 2:

                    @pl.when(step + 1 < far)
                    def _():
                        relay_piece(side, step, 1, p)

        if far > 1:
            if far == 2:
                relay_fine(step)
            else:

                @pl.when(step + 1 == far)
                def _():
                    relay_fine(step)

    take_values(1)
    blend(1)

    if far > 2:

        @pl.loop(2, far)
        def _(step):
            for p in range(parts):
                take(step, 0, p)
            take_values(step)
            blend(step)

    if far > 1:
        for p in range(parts):
            for side in (LEFT, RIGHT):
                await_piece(side, far, 0, p)

    def last(h):
        if far > 1:
            for side in (LEFT, RIGHT):

                @pl.when(gets(side, far))
                def _():
                    weights, keep = masked(h, source(side, far))
                    wb[side] = weights
                    acc[h] = acc[h] * keep

        if far > 1:
            for side in (LEFT, RIGHT):

                @pl.when(gets(side, far))
                def _():
                    fine(side, h, back=True).wait_recv()
                    acc[h] = acc[h] + mixed(wb[side], h, source(side, far))

        result = jnp.transpose(acc[h] * (1.0 / total[h])).astype(jnp.bfloat16)
        ob[:, :, lane(h)] = result.reshape(parts, rows, HEAD_DIM)
        for j in range(1, parts):
            o_exchange(h, j).start()
        out_ref[:, lane(part * heads + h)] = ob[part, :, lane(h)]

    each_head(last)

    def close_head(h):
        for j in range(1, parts):
            o_exchange(h, j).wait()
        if far > 1:
            for side in (LEFT, RIGHT):

                @pl.when(can_send(side, far))
                def _():
                    fine(side, h).wait_send()

    for i in range(3):
        for j in range(1, parts):
            exchange(j, i).wait_send()

    @pl.loop(1, far + 1)
    def _(step):
        for side in (LEFT, RIGHT):

            @pl.when(can_send(side, step))
            def _():
                for p in range(parts):
                    hop(side, step, 0, p).wait_send()

                    @pl.when((step < far) | (step == 1))
                    def _():
                        hop(side, step, 1, p).wait_send()

    each_head(close_head)


def shards(frames, parts, queries, keys, values, flags, widths):
    shape = queries.shape
    columns, features = shape[2], shape[3]
    rows = shape[1] * columns
    heads = features // HEAD_DIM // parts
    tokens = rows * parts
    far = frames - 2
    flat = [a.reshape(rows, features) for a in (queries, keys, values)]
    any_spec = pl.BlockSpec(memory_space=pl.ANY)
    others = max(parts - 1, 1)
    dma = pltpu.SemaphoreType.DMA
    out = pl.pallas_call(
        functools.partial(kernel, frames, parts, heads, columns),
        out_shape=pltpu.VMEM((rows, features), jnp.bfloat16),
        in_specs=[any_spec] * 5,
        out_specs=pl.BlockSpec(memory_space=pltpu.VMEM),
        scratch_shapes=[
            pltpu.VMEM((frames, 2, parts, rows, heads * HEAD_DIM), jnp.bfloat16),
            pltpu.VMEM((parts, rows, heads * HEAD_DIM), jnp.bfloat16),
            pltpu.VMEM((parts, rows, heads * HEAD_DIM), jnp.bfloat16),
            pltpu.VMEM((tokens, tokens), jnp.float32),
            pltpu.VMEM((2, tokens, tokens), jnp.bfloat16),
            pltpu.VMEM((heads, 1, tokens), jnp.float32),
            pltpu.VMEM((heads, 1, tokens), jnp.float32),
            pltpu.VMEM((heads, HEAD_DIM, tokens), jnp.float32),
            dma((3,)),
            dma((3, others)),
            dma((3, others)),
            dma((2, far, 2, parts)),
            dma((2, far, 2, parts)),
            dma((2, heads)),
            dma((2, heads)),
            dma((others, heads)),
            dma((others, heads)),
            pltpu.SMEM(flags.shape, jnp.int32),
            pltpu.SMEM(widths.shape, jnp.int32),
            dma((2,)),
        ],
        compiler_params=pltpu.CompilerParams(collective_id=0, has_side_effects=True),
    )(*flat, flags, widths)
    return out.reshape(shape)


def solution(mesh):
    spec = P(("group", "frame"), "space", None, "head")
    return jax.shard_map(
        functools.partial(shards, mesh.shape["frame"], mesh.shape["space"]),
        mesh=mesh,
        in_specs=(spec, spec, spec, P(), P()),
        out_specs=spec,
        check_vma=False,
    )
```

```python
import functools
import math

import jax
import jax.numpy as jnp
from jax import lax
from jax.experimental import pallas as pl
from jax.experimental.pallas import tpu as pltpu
from jax.sharding import PartitionSpec as P

HEAD_DIM = 128
NEG_FILL = -1e30
SCALE = math.log2(math.e) / HEAD_DIM**0.5
MESH = pl.DeviceIdType.MESH
LEFT, RIGHT = 0, 1


def kernel(
    frames,
    parts,
    heads,
    columns,
    q_ref,
    k_ref,
    v_ref,
    flags_in,
    widths_in,
    out_ref,
    kv,
    qb,
    ob,
    dist,
    wb,
    top,
    total,
    acc,
    local_sem,
    x_send,
    x_recv,
    z_send,
    z_recv,
    f_send,
    f_recv,
    o_send,
    o_recv,
    flags_ref,
    widths_ref,
    table_sem,
):
    frame = lax.axis_index("frame")
    part = lax.axis_index("space")
    rows = q_ref.shape[0]
    tokens = parts * rows
    width = heads * HEAD_DIM
    far = frames - 2
    inputs = (k_ref, v_ref, q_ref)

    def lane(head):
        return pl.ds(pl.multiple_of(head * HEAD_DIM, HEAD_DIM), HEAD_DIM)

    def span(p):
        return pl.ds(pl.multiple_of(p * width, HEAD_DIM), width)

    def peer(j):
        return lax.rem(part + j, parts)

    def home(i):
        return qb.at[part] if i == 2 else kv.at[frame, i, part]

    barrier = pltpu.get_barrier_semaphore()
    for j in range(1, parts):
        pl.semaphore_signal(barrier, inc=1, device_id={"space": peer(j)}, device_id_type=MESH)

    @pl.when(frame > 0)
    def _():
        pl.semaphore_signal(barrier, inc=1, device_id={"frame": frame - 1}, device_id_type=MESH)

    @pl.when(frame < frames - 1)
    def _():
        pl.semaphore_signal(barrier, inc=1, device_id={"frame": frame + 1}, device_id_type=MESH)

    def local_copy(i):
        return pltpu.make_async_copy(inputs[i].at[:, span(part)], home(i), local_sem.at[i])

    def exchange(j, i):
        return pltpu.make_async_remote_copy(
            src_ref=inputs[i].at[:, span(peer(j))],
            dst_ref=home(i),
            send_sem=x_send.at[i, j - 1],
            recv_sem=x_recv.at[i, j - 1],
            device_id={"space": peer(j)},
            device_id_type=MESH,
        )

    def o_exchange(h, j):
        return pltpu.make_async_remote_copy(
            src_ref=ob.at[peer(j), :, lane(h)],
            dst_ref=out_ref.at[:, lane(part * heads + h)],
            send_sem=o_send.at[j - 1, h],
            recv_sem=o_recv.at[j - 1, h],
            device_id={"space": peer(j)},
            device_id_type=MESH,
        )

    def towards(side):
        return 1 if side == RIGHT else -1

    def hop(side, step, i, p, src=None, back=False):
        ahead = towards(side)
        owner = frame - ahead * (step if back else step - 1)
        block = kv.at[owner, i, p]
        return pltpu.make_async_remote_copy(
            src_ref=block if src is None else src,
            dst_ref=block,
            send_sem=z_send.at[side, step - 1, i, p],
            recv_sem=z_recv.at[side, step - 1, i, p],
            device_id={"frame": frame - ahead if back else frame + ahead},
            device_id_type=MESH,
        )

    def fine(side, h, back=False):
        ahead = towards(side)
        owner = frame - ahead * (far if back else far - 1)
        block = kv.at[owner, 1, :, :, lane(h)]
        return pltpu.make_async_remote_copy(
            src_ref=block,
            dst_ref=block,
            send_sem=f_send.at[side, h],
            recv_sem=f_recv.at[side, h],
            device_id={"frame": frame - ahead if back else frame + ahead},
            device_id_type=MESH,
        )

    def can_send(side, step):
        if side == RIGHT:
            return (frame < frames - 1) & (frame - (step - 1) >= 0)
        return (frame > 0) & (frame + (step - 1) <= frames - 1)

    def gets(side, step):
        if side == RIGHT:
            return frame - step >= 0
        return frame + step <= frames - 1

    def source(side, step):
        return frame - step if side == RIGHT else frame + step

    def each_head(body):
        @pl.loop(0, heads)
        def _(h):
            body(h)

    pl.semaphore_wait(
        barrier,
        parts - 1 + jnp.where(frame > 0, 1, 0) + jnp.where(frame < frames - 1, 1, 0),
    )

    for i in (0, 1):
        for j in range(1, parts):
            exchange(j, i).start()
        for side in (LEFT, RIGHT):

            @pl.when(can_send(side, 1))
            def _():
                hop(side, 1, i, part, inputs[i].at[:, span(part)]).start()

    tables = (
        pltpu.make_async_copy(flags_in, flags_ref, table_sem.at[0]),
        pltpu.make_async_copy(widths_in, widths_ref, table_sem.at[1]),
    )
    for copy in tables:
        copy.start()
    for i in range(3):
        local_copy(i).start()
    for j in range(1, parts):
        exchange(j, 2).start()

    def row_of(axis):
        at = lax.broadcasted_iota(jnp.int32, (tokens, tokens), axis).astype(jnp.float32)
        return jnp.floor((at + 0.5) * (1.0 / columns))

    dist[...] = jnp.abs(row_of(0) - row_of(1))
    top[...] = jnp.full(top.shape, NEG_FILL, jnp.float32)
    total[...] = jnp.zeros(total.shape, jnp.float32)
    acc[...] = jnp.zeros(acc.shape, jnp.float32)

    def await_piece(side, step, i, p):
        @pl.when(gets(side, step))
        def _():
            hop(side, step, i, p, back=True).wait_recv()

    def relay_piece(side, step, i, p):
        @pl.when(gets(side, step) & can_send(side, step + 1))
        def _():
            hop(side, step + 1, i, p).start()

    def relay_fine(step):
        for side in (LEFT, RIGHT):

            @pl.when(gets(side, step) & can_send(side, step + 1))
            def _():
                each_head(lambda h: fine(side, h).start())

    def pass_piece(i):
        for j in range(1, parts):
            p = lax.rem(part - j + parts, parts)
            exchange(j, i).wait_recv()
            for side in (LEFT, RIGHT):

                @pl.when(can_send(side, 1))
                def _():
                    hop(side, 1, i, p).start()

    def take(step, i, p):
        for side in (LEFT, RIGHT):
            await_piece(side, step, i, p)
            if far > 1:
                relay_piece(side, step, i, p)

    pass_piece(0)
    take(1, 0, part)
    pass_piece(1)
    for copy in tables:
        copy.wait()

    def masked(h, g):
        gap = jnp.abs(frame - g)
        reach = jnp.where(flags_ref[frame, g] > 0, widths_ref[gap], -1).astype(jnp.float32)
        keys = kv[g, 0, :, :, lane(h)].reshape(tokens, HEAD_DIM)
        queries = qb[:, :, lane(h)].reshape(tokens, HEAD_DIM)
        scores = lax.dot_general(
            keys, queries, (((1,), (1,)), ((), ())), preferred_element_type=jnp.float32
        )
        scores = jnp.where(dist[...] <= reach, scores, NEG_FILL)
        old_top = top[h]
        new_top = jnp.maximum(old_top, jnp.max(scores, axis=0, keepdims=True))
        weights = jnp.exp2((scores - new_top) * SCALE)
        keep = jnp.exp2((old_top - new_top) * SCALE)
        top[h] = new_top
        total[h] = total[h] * keep + jnp.sum(weights, axis=0, keepdims=True)
        return weights.astype(jnp.bfloat16), keep

    def mixed(weights, h, g):
        vals = kv[g, 1, :, :, lane(h)].reshape(tokens, HEAD_DIM)
        return lax.dot_general(
            vals, weights, (((0,), (0,)), ((), ())), preferred_element_type=jnp.float32
        )

    def update(h, g):
        weights, keep = masked(h, g)
        acc[h] = acc[h] * keep + mixed(weights, h, g)

    def blend(step):
        def body(h):
            for side in (LEFT, RIGHT):

                @pl.when(gets(side, step))
                def _():
                    update(h, source(side, step))

        each_head(body)

    for j in range(1, parts):
        take(1, 0, peer(j))
    for i in range(3):
        local_copy(i).wait()
    for j in range(1, parts):
        exchange(j, 2).wait_recv()
    each_head(lambda h: update(h, frame))

    def take_values(step):
        for p in range(parts):
            for side in (LEFT, RIGHT):
                await_piece(side, step, 1, p)
                if far > 2:

                    @pl.when(step + 1 < far)
                    def _():
                        relay_piece(side, step, 1, p)

        if far > 1:
            if far == 2:
                relay_fine(step)
            else:

                @pl.when(step + 1 == far)
                def _():
                    relay_fine(step)

    take_values(1)
    blend(1)

    if far > 2:

        @pl.loop(2, far)
        def _(step):
            for p in range(parts):
                take(step, 0, p)
            take_values(step)
            blend(step)

    if far > 1:
        for p in range(parts):
            for side in (LEFT, RIGHT):
                await_piece(side, far, 0, p)

    def last(h):
        if far > 1:
            for side in (LEFT, RIGHT):

                @pl.when(gets(side, far))
                def _():
                    weights, keep = masked(h, source(side, far))
                    wb[side] = weights
                    acc[h] = acc[h] * keep

        if far > 1:
            for side in (LEFT, RIGHT):

                @pl.when(gets(side, far))
                def _():
                    fine(side, h, back=True).wait_recv()
                    acc[h] = acc[h] + mixed(wb[side], h, source(side, far))

        result = jnp.transpose(acc[h] * (1.0 / total[h])).astype(jnp.bfloat16)
        ob[:, :, lane(h)] = result.reshape(parts, rows, HEAD_DIM)
        for j in range(1, parts):
            o_exchange(h, j).start()
        out_ref[:, lane(part * heads + h)] = ob[part, :, lane(h)]

    each_head(last)

    def close_head(h):
        for j in range(1, parts):
            o_exchange(h, j).wait()
        if far > 1:
            for side in (LEFT, RIGHT):

                @pl.when(can_send(side, far))
                def _():
                    fine(side, h).wait_send()

    for i in range(3):
        for j in range(1, parts):
            exchange(j, i).wait_send()

    @pl.loop(1, far + 1)
    def _(step):
        for side in (LEFT, RIGHT):

            @pl.when(can_send(side, step))
            def _():
                for p in range(parts):
                    hop(side, step, 0, p).wait_send()

                    @pl.when((step < far) | (step == 1))
                    def _():
                        hop(side, step, 1, p).wait_send()

    each_head(close_head)


def head_groups(heads):
    edges = list(range(0, max(heads - 2, 0), 2)) + [h for h in (heads - 2, heads - 1) if h >= 0]
    return list(zip(edges, edges[1:] + [heads]))


def helped_kernel(
    frames,
    parts,
    heads,
    columns,
    skip,
    q_ref,
    k_ref,
    v_ref,
    flags_in,
    widths_in,
    out_ref,
    kvq,
    given,
    given_stat,
    got,
    got_stat,
    ob,
    dist,
    top,
    total,
    acc,
    local_sem,
    x_send,
    x_recv,
    n_send,
    n_recv,
    p_send,
    p_recv,
    a_send,
    a_recv,
    s_send,
    s_recv,
    o_send,
    o_recv,
    flags_ref,
    widths_ref,
    table_sem,
):
    frame = lax.axis_index("frame")
    part = lax.axis_index("space")
    rows = q_ref.shape[0]
    tokens = parts * rows
    inputs = (k_ref, v_ref, q_ref)
    groups = head_groups(heads)
    lag = min(2, heads)

    def lane(head, count=1):
        return pl.ds(pl.multiple_of(head * HEAD_DIM, HEAD_DIM), count * HEAD_DIM)

    def piece(gi, p=None):
        low, high = groups[gi]
        return lane(low if p is None else p * heads + low, high - low)

    def peer(j):
        return lax.rem(part + j, parts)

    def giver(j):
        return lax.rem(part - j + parts, parts)

    def ahead(side):
        return 1 if side == RIGHT else -1

    def inner(helper, side):
        here = (helper >= 1) & (helper <= frames - 2)
        return here & (helper != skip[1]) if side == skip[0] else here

    def helps(side):
        return inner(frame, side)

    def asks(side):
        return inner(frame - ahead(side), side) & (frame >= 0)

    def has(side):
        return frame < frames - 1 if side == RIGHT else frame > 0

    def near(side):
        return frame > 0 if side == RIGHT else frame < frames - 1

    barrier = pltpu.get_barrier_semaphore()
    for j in range(1, parts):
        pl.semaphore_signal(barrier, inc=1, device_id={"space": peer(j)}, device_id_type=MESH)
    for side in (LEFT, RIGHT):

        @pl.when(has(side))
        def _():
            pl.semaphore_signal(
                barrier, inc=1, device_id={"frame": frame + ahead(side)}, device_id_type=MESH
            )

    pl.semaphore_wait(
        barrier,
        parts - 1 + jnp.where(frame > 0, 1, 0) + jnp.where(frame < frames - 1, 1, 0),
    )

    def local_copy(i):
        return pltpu.make_async_copy(
            inputs[i].at[:, lane(part * heads, heads)], kvq.at[frame, i, part], local_sem.at[i]
        )

    def exchange(j, i, gi):
        return pltpu.make_async_remote_copy(
            src_ref=inputs[i].at[:, piece(gi, peer(j))],
            dst_ref=kvq.at[frame, i, part, :, piece(gi)],
            send_sem=x_send.at[i, j - 1, gi],
            recv_sem=x_recv.at[i, j - 1, gi],
            device_id={"space": peer(j)},
            device_id_type=MESH,
        )

    def own_hop(side, i, gi, back=False):
        owner = frame - ahead(side) if back else frame
        return pltpu.make_async_remote_copy(
            src_ref=inputs[i].at[:, piece(gi, part)],
            dst_ref=kvq.at[owner, i, part, :, piece(gi)],
            send_sem=n_send.at[side, i, gi],
            recv_sem=n_recv.at[side, i, gi],
            device_id={"frame": owner if back else frame + ahead(side)},
            device_id_type=MESH,
        )

    def pass_hop(side, p, j, gi, count, back=False):
        owner = frame - ahead(side) if back else frame
        block = kvq.at[owner, pl.ds(0, count), p, :, piece(gi)]
        return pltpu.make_async_remote_copy(
            src_ref=block,
            dst_ref=block,
            send_sem=p_send.at[side, j - 1, gi],
            recv_sem=p_recv.at[side, j - 1, gi],
            device_id={"frame": owner if back else frame + ahead(side)},
            device_id_type=MESH,
        )

    def answer(side, h, back=False):
        to = frame - ahead(side) if back else frame + ahead(side)
        return tuple(
            pltpu.make_async_remote_copy(
                src_ref=src.at[side, h],
                dst_ref=dst.at[side, h],
                send_sem=send.at[side, h],
                recv_sem=recv.at[side, h],
                device_id={"frame": to},
                device_id_type=MESH,
            )
            for src, dst, send, recv in (
                (given, got, a_send, a_recv),
                (given_stat, got_stat, s_send, s_recv),
            )
        )

    def o_exchange(h, j):
        return pltpu.make_async_remote_copy(
            src_ref=ob.at[peer(j), :, lane(h)],
            dst_ref=out_ref.at[:, lane(part * heads + h)],
            send_sem=o_send.at[j - 1, h],
            recv_sem=o_recv.at[j - 1, h],
            device_id={"space": peer(j)},
            device_id_type=MESH,
        )

    def opposite(side):
        return LEFT if side == RIGHT else RIGHT

    def start_own(gi):
        for i in (2, 0, 1):
            for side in (LEFT, RIGHT):
                wanted = has(side) & asks(opposite(side)) if i == 2 else has(side)

                @pl.when(wanted)
                def _():
                    own_hop(side, i, gi).start()

    def each_pass(gi, act):
        for j in range(1, parts):
            for side in (LEFT, RIGHT):
                for count in (2, 3):
                    query = asks(opposite(side))

                    @pl.when(has(side) & (query if count == 3 else jnp.logical_not(query)))
                    def _():
                        act(pass_hop(side, giver(j), j, gi, count))

    def forward(gi):
        for j in range(1, parts):
            for i in range(3):
                exchange(j, i, gi).wait_recv()
        each_pass(gi, lambda copy: copy.start())

    order = list(range(len(groups)))
    for j in range(1, parts):
        for i in range(3):
            exchange(j, i, 0).start()
    start_own(0)
    if len(groups) > 1:
        start_own(order[-1])
    for gi in order[1:]:
        for j in range(1, parts):
            for i in range(3):
                exchange(j, i, gi).start()
    tables = (
        pltpu.make_async_copy(flags_in, flags_ref, table_sem.at[0]),
        pltpu.make_async_copy(widths_in, widths_ref, table_sem.at[1]),
    )
    for copy in tables:
        copy.start()
    for i in range(3):
        local_copy(i).start()

    def row_of(axis):
        at = lax.broadcasted_iota(jnp.int32, (tokens, tokens), axis).astype(jnp.float32)
        return jnp.floor((at + 0.5) * (1.0 / columns))

    dist[...] = jnp.abs(row_of(0) - row_of(1))
    top[...] = jnp.full(top.shape, NEG_FILL, jnp.float32)
    total[...] = jnp.zeros(total.shape, jnp.float32)
    acc[...] = jnp.zeros(acc.shape, jnp.float32)
    for copy in tables:
        copy.wait()
    for i in range(3):
        local_copy(i).wait()

    for gi in order[:-1]:
        forward(gi)
        if gi + 1 < len(groups) - 1:
            start_own(gi + 1)
    forward(order[-1])

    def await_group(gi):
        for side in (LEFT, RIGHT):
            for i in (2, 0, 1):

                @pl.when(near(side) & helps(opposite(side)) if i == 2 else near(side))
                def _():
                    own_hop(side, i, gi, back=True).wait_recv()

            for j in range(1, parts):
                for count in (2, 3):
                    query = helps(opposite(side))

                    @pl.when(near(side) & (query if count == 3 else jnp.logical_not(query)))
                    def _():
                        pass_hop(side, giver(j), j, gi, count, back=True).wait_recv()

    def whole(f, i, h):
        return kvq[f, i, :, :, lane(h)].reshape(tokens, HEAD_DIM)

    def scores_of(h, f, g):
        gap = jnp.abs(f - g)
        reach = jnp.where(flags_ref[f, g] > 0, widths_ref[gap], -1).astype(jnp.float32)
        scores = lax.dot_general(
            whole(g, 0, h),
            whole(f, 2, h),
            (((1,), (1,)), ((), ())),
            preferred_element_type=jnp.float32,
        )
        return jnp.where(dist[...] <= reach, scores, NEG_FILL)

    def mixed(weights, h, g):
        return lax.dot_general(
            whole(g, 1, h),
            weights.astype(jnp.bfloat16),
            (((0,), (0,)), ((), ())),
            preferred_element_type=jnp.float32,
        )

    def update(h, g):
        scores = scores_of(h, frame, g)
        old_top = top[h]
        new_top = jnp.maximum(old_top, jnp.max(scores, axis=0, keepdims=True))
        weights = jnp.exp2((scores - new_top) * SCALE)
        keep = jnp.exp2((old_top - new_top) * SCALE)
        top[h] = new_top
        total[h] = total[h] * keep + jnp.sum(weights, axis=0, keepdims=True)
        acc[h] = acc[h] * keep + mixed(weights, h, g)

    def help_with(side, h):
        f, g = frame + ahead(side), frame - ahead(side)
        scores = scores_of(h, f, g)
        peak = jnp.max(scores, axis=0, keepdims=True)
        weights = jnp.exp2((scores - peak) * SCALE)
        given_stat[side, h, 0:1] = peak
        given_stat[side, h, 1:2] = jnp.sum(weights, axis=0, keepdims=True)
        given[side, h] = mixed(weights, h, g).astype(jnp.bfloat16)
        for copy in answer(side, h):
            copy.start()

    def compute(h):
        for gi, (low, _high) in enumerate(groups):

            @pl.when(h == low)
            def _():
                await_group(gi)

        for side in (LEFT, RIGHT):

            @pl.when(helps(side))
            def _():
                help_with(side, h)

        update(h, frame)
        for side in (LEFT, RIGHT):

            @pl.when(near(side))
            def _():
                update(h, frame - ahead(side))

    def finish(h):
        for side in (LEFT, RIGHT):

            @pl.when(asks(side))
            def _():
                for copy in answer(side, h, back=True):
                    copy.wait_recv()
                peak = got_stat[side, h, 0:1]
                new_top = jnp.maximum(top[h], peak)
                keep = jnp.exp2((top[h] - new_top) * SCALE)
                add = jnp.exp2((peak - new_top) * SCALE)
                total[h] = total[h] * keep + got_stat[side, h, 1:2] * add
                acc[h] = acc[h] * keep + got[side, h].astype(jnp.float32) * add

        result = jnp.transpose(acc[h] * (1.0 / total[h])).astype(jnp.bfloat16)
        ob[:, :, lane(h)] = result.reshape(parts, rows, HEAD_DIM)
        for j in range(1, parts):
            o_exchange(h, j).start()
        out_ref[:, lane(part * heads + h)] = ob[part, :, lane(h)]

    @pl.loop(0, heads + lag)
    def _(step):
        @pl.when(step < heads)
        def _():
            compute(step)

        @pl.when(step >= lag)
        def _():
            finish(step - lag)

    for gi in order:
        for j in range(1, parts):
            for i in range(3):
                exchange(j, i, gi).wait_send()
        for i in (2, 0, 1):
            for side in (LEFT, RIGHT):
                wanted = has(side) & asks(opposite(side)) if i == 2 else has(side)

                @pl.when(wanted)
                def _():
                    own_hop(side, i, gi).wait_send()

        each_pass(gi, lambda copy: copy.wait_send())

    @pl.loop(0, heads)
    def _(h):
        for side in (LEFT, RIGHT):

            @pl.when(helps(side))
            def _():
                for copy in answer(side, h):
                    copy.wait_send()

        for j in range(1, parts):
            o_exchange(h, j).wait()


def choose_kernel(frames, flags_ref, index_ref):
    right = flags_ref[frames - 2, 0] > 0
    left = flags_ref[1, frames - 1] > 0
    index_ref[0] = jnp.where(left, jnp.where(right, 0, 2), 1)


def shards(frames, parts, queries, keys, values, flags, widths):
    shape = queries.shape
    columns, features = shape[2], shape[3]
    rows = shape[1] * columns
    heads = features // HEAD_DIM // parts
    tokens = rows * parts
    far = frames - 2
    flat = [a.reshape(rows, features) for a in (queries, keys, values)]
    any_spec = pl.BlockSpec(memory_space=pl.ANY)
    others = max(parts - 1, 1)
    dma = pltpu.SemaphoreType.DMA
    vmem = pltpu.VMEM
    width = heads * HEAD_DIM
    tables = [pltpu.SMEM(flags.shape, jnp.int32), pltpu.SMEM(widths.shape, jnp.int32), dma((2,))]
    common = dict(
        out_shape=vmem((rows, features), jnp.bfloat16),
        in_specs=[any_spec] * 5,
        out_specs=pl.BlockSpec(memory_space=vmem),
    )

    def full(*operands):
        return pl.pallas_call(
            functools.partial(kernel, frames, parts, heads, columns),
            scratch_shapes=[
                vmem((frames, 2, parts, rows, width), jnp.bfloat16),
                vmem((parts, rows, width), jnp.bfloat16),
                vmem((parts, rows, width), jnp.bfloat16),
                vmem((tokens, tokens), jnp.float32),
                vmem((2, tokens, tokens), jnp.bfloat16),
                vmem((heads, 1, tokens), jnp.float32),
                vmem((heads, 1, tokens), jnp.float32),
                vmem((heads, HEAD_DIM, tokens), jnp.float32),
                dma((3,)),
                dma((3, others)),
                dma((3, others)),
                dma((2, far, 2, parts)),
                dma((2, far, 2, parts)),
                dma((2, heads)),
                dma((2, heads)),
                dma((others, heads)),
                dma((others, heads)),
            ]
            + tables,
            compiler_params=pltpu.CompilerParams(collective_id=0, has_side_effects=True),
            name="full",
            **common,
        )(*operands)

    def helped(skip, collective_id):
        pieces = len(head_groups(heads))

        def call(*operands):
            return pl.pallas_call(
                functools.partial(helped_kernel, frames, parts, heads, columns, skip),
                scratch_shapes=[
                    vmem((frames, 3, parts, rows, width), jnp.bfloat16),
                    vmem((2, heads, HEAD_DIM, tokens), jnp.bfloat16),
                    vmem((2, heads, 8, tokens), jnp.float32),
                    vmem((2, heads, HEAD_DIM, tokens), jnp.bfloat16),
                    vmem((2, heads, 8, tokens), jnp.float32),
                    vmem((parts, rows, width), jnp.bfloat16),
                    vmem((tokens, tokens), jnp.float32),
                    vmem((heads, 1, tokens), jnp.float32),
                    vmem((heads, 1, tokens), jnp.float32),
                    vmem((heads, HEAD_DIM, tokens), jnp.float32),
                    dma((3,)),
                    dma((3, others, pieces)),
                    dma((3, others, pieces)),
                    dma((2, 3, pieces)),
                    dma((2, 3, pieces)),
                    dma((2, others, pieces)),
                    dma((2, others, pieces)),
                    dma((2, heads)),
                    dma((2, heads)),
                    dma((2, heads)),
                    dma((2, heads)),
                    dma((others, heads)),
                    dma((others, heads)),
                ]
                + tables,
                compiler_params=pltpu.CompilerParams(
                    collective_id=collective_id, has_side_effects=True
                ),
                name=f"helped{collective_id}",
                **common,
            )(*operands)

        return call

    operands = (*flat, flags, widths)
    if far == 2:
        index = pl.pallas_call(
            functools.partial(choose_kernel, frames),
            out_shape=pltpu.SMEM((1,), jnp.int32),
            in_specs=[pl.BlockSpec(memory_space=pltpu.SMEM)],
            out_specs=pl.BlockSpec(memory_space=pltpu.SMEM),
            name="choose",
        )(flags)
        branches = [full, helped((LEFT, frames - 2), 1), helped((RIGHT, 1), 2)]
        out = lax.switch(index[0], branches, *operands)
    else:
        out = full(*operands)
    return out.reshape(shape)


def solution(mesh):
    spec = P(("group", "frame"), "space", None, "head")
    return jax.shard_map(
        functools.partial(shards, mesh.shape["frame"], mesh.shape["space"]),
        mesh=mesh,
        in_specs=(spec, spec, spec, P(), P()),
        out_specs=spec,
        check_vma=False,
    )
```

```python
import functools
import math

import jax
import jax.numpy as jnp
from jax import lax
from jax.experimental import pallas as pl
from jax.experimental.pallas import tpu as pltpu
from jax.sharding import PartitionSpec as P

HEAD_DIM = 128
NEG_FILL = -1e30
SCALE = math.log2(math.e) / HEAD_DIM**0.5
MESH = pl.DeviceIdType.MESH
LEFT, RIGHT = 0, 1


def kernel(
    frames,
    parts,
    heads,
    columns,
    q_ref,
    k_ref,
    v_ref,
    flags_in,
    widths_in,
    out_ref,
    kv,
    qb,
    ob,
    dist,
    wb,
    top,
    total,
    acc,
    local_sem,
    x_send,
    x_recv,
    z_send,
    z_recv,
    f_send,
    f_recv,
    o_send,
    o_recv,
    flags_ref,
    widths_ref,
    table_sem,
):
    frame = lax.axis_index("frame")
    part = lax.axis_index("space")
    rows = q_ref.shape[0]
    tokens = parts * rows
    width = heads * HEAD_DIM
    far = frames - 2
    inputs = (k_ref, v_ref, q_ref)

    def lane(head):
        return pl.ds(pl.multiple_of(head * HEAD_DIM, HEAD_DIM), HEAD_DIM)

    def span(p):
        return pl.ds(pl.multiple_of(p * width, HEAD_DIM), width)

    def peer(j):
        return lax.rem(part + j, parts)

    def home(i):
        return qb.at[part] if i == 2 else kv.at[frame, i, part]

    barrier = pltpu.get_barrier_semaphore()
    for j in range(1, parts):
        pl.semaphore_signal(barrier, inc=1, device_id={"space": peer(j)}, device_id_type=MESH)

    @pl.when(frame > 0)
    def _():
        pl.semaphore_signal(barrier, inc=1, device_id={"frame": frame - 1}, device_id_type=MESH)

    @pl.when(frame < frames - 1)
    def _():
        pl.semaphore_signal(barrier, inc=1, device_id={"frame": frame + 1}, device_id_type=MESH)

    def local_copy(i):
        return pltpu.make_async_copy(inputs[i].at[:, span(part)], home(i), local_sem.at[i])

    def exchange(j, i):
        return pltpu.make_async_remote_copy(
            src_ref=inputs[i].at[:, span(peer(j))],
            dst_ref=home(i),
            send_sem=x_send.at[i, j - 1],
            recv_sem=x_recv.at[i, j - 1],
            device_id={"space": peer(j)},
            device_id_type=MESH,
        )

    def o_exchange(h, j):
        return pltpu.make_async_remote_copy(
            src_ref=ob.at[peer(j), :, lane(h)],
            dst_ref=out_ref.at[:, lane(part * heads + h)],
            send_sem=o_send.at[j - 1, h],
            recv_sem=o_recv.at[j - 1, h],
            device_id={"space": peer(j)},
            device_id_type=MESH,
        )

    def towards(side):
        return 1 if side == RIGHT else -1

    def hop(side, step, i, p, src=None, back=False):
        ahead = towards(side)
        owner = frame - ahead * (step if back else step - 1)
        block = kv.at[owner, i, p]
        return pltpu.make_async_remote_copy(
            src_ref=block if src is None else src,
            dst_ref=block,
            send_sem=z_send.at[side, step - 1, i, p],
            recv_sem=z_recv.at[side, step - 1, i, p],
            device_id={"frame": frame - ahead if back else frame + ahead},
            device_id_type=MESH,
        )

    def fine(side, h, back=False):
        ahead = towards(side)
        owner = frame - ahead * (far if back else far - 1)
        block = kv.at[owner, 1, :, :, lane(h)]
        return pltpu.make_async_remote_copy(
            src_ref=block,
            dst_ref=block,
            send_sem=f_send.at[side, h],
            recv_sem=f_recv.at[side, h],
            device_id={"frame": frame - ahead if back else frame + ahead},
            device_id_type=MESH,
        )

    def can_send(side, step):
        if side == RIGHT:
            return (frame < frames - 1) & (frame - (step - 1) >= 0)
        return (frame > 0) & (frame + (step - 1) <= frames - 1)

    def gets(side, step):
        if side == RIGHT:
            return frame - step >= 0
        return frame + step <= frames - 1

    def source(side, step):
        return frame - step if side == RIGHT else frame + step

    def each_head(body):
        @pl.loop(0, heads)
        def _(h):
            body(h)

    pl.semaphore_wait(
        barrier,
        parts - 1 + jnp.where(frame > 0, 1, 0) + jnp.where(frame < frames - 1, 1, 0),
    )

    for i in (0, 1):
        for j in range(1, parts):
            exchange(j, i).start()
        for side in (LEFT, RIGHT):

            @pl.when(can_send(side, 1))
            def _():
                hop(side, 1, i, part, inputs[i].at[:, span(part)]).start()

    tables = (
        pltpu.make_async_copy(flags_in, flags_ref, table_sem.at[0]),
        pltpu.make_async_copy(widths_in, widths_ref, table_sem.at[1]),
    )
    for copy in tables:
        copy.start()
    for i in range(3):
        local_copy(i).start()
    for j in range(1, parts):
        exchange(j, 2).start()

    def row_of(axis):
        at = lax.broadcasted_iota(jnp.int32, (tokens, tokens), axis).astype(jnp.float32)
        return jnp.floor((at + 0.5) * (1.0 / columns))

    dist[...] = jnp.abs(row_of(0) - row_of(1))
    top[...] = jnp.full(top.shape, NEG_FILL, jnp.float32)
    total[...] = jnp.zeros(total.shape, jnp.float32)
    acc[...] = jnp.zeros(acc.shape, jnp.float32)

    def await_piece(side, step, i, p):
        @pl.when(gets(side, step))
        def _():
            hop(side, step, i, p, back=True).wait_recv()

    def relay_piece(side, step, i, p):
        @pl.when(gets(side, step) & can_send(side, step + 1))
        def _():
            hop(side, step + 1, i, p).start()

    def relay_fine(step):
        for side in (LEFT, RIGHT):

            @pl.when(gets(side, step) & can_send(side, step + 1))
            def _():
                each_head(lambda h: fine(side, h).start())

    def pass_piece(i):
        for j in range(1, parts):
            p = lax.rem(part - j + parts, parts)
            exchange(j, i).wait_recv()
            for side in (LEFT, RIGHT):

                @pl.when(can_send(side, 1))
                def _():
                    hop(side, 1, i, p).start()

    def take(step, i, p):
        for side in (LEFT, RIGHT):
            await_piece(side, step, i, p)
            if far > 1:
                relay_piece(side, step, i, p)

    pass_piece(0)
    take(1, 0, part)
    pass_piece(1)
    for copy in tables:
        copy.wait()

    def masked(h, g):
        gap = jnp.abs(frame - g)
        reach = jnp.where(flags_ref[frame, g] > 0, widths_ref[gap], -1).astype(jnp.float32)
        keys = kv[g, 0, :, :, lane(h)].reshape(tokens, HEAD_DIM)
        queries = qb[:, :, lane(h)].reshape(tokens, HEAD_DIM)
        scores = lax.dot_general(
            keys, queries, (((1,), (1,)), ((), ())), preferred_element_type=jnp.float32
        )
        scores = jnp.where(dist[...] <= reach, scores, NEG_FILL)
        old_top = top[h]
        new_top = jnp.maximum(old_top, jnp.max(scores, axis=0, keepdims=True))
        weights = jnp.exp2((scores - new_top) * SCALE)
        keep = jnp.exp2((old_top - new_top) * SCALE)
        top[h] = new_top
        total[h] = total[h] * keep + jnp.sum(weights, axis=0, keepdims=True)
        return weights.astype(jnp.bfloat16), keep

    def mixed(weights, h, g):
        vals = kv[g, 1, :, :, lane(h)].reshape(tokens, HEAD_DIM)
        return lax.dot_general(
            vals, weights, (((0,), (0,)), ((), ())), preferred_element_type=jnp.float32
        )

    def update(h, g):
        weights, keep = masked(h, g)
        acc[h] = acc[h] * keep + mixed(weights, h, g)

    def blend(step):
        def body(h):
            for side in (LEFT, RIGHT):

                @pl.when(gets(side, step))
                def _():
                    update(h, source(side, step))

        each_head(body)

    for j in range(1, parts):
        take(1, 0, peer(j))
    for i in range(3):
        local_copy(i).wait()
    for j in range(1, parts):
        exchange(j, 2).wait_recv()
    each_head(lambda h: update(h, frame))

    def take_values(step):
        for p in range(parts):
            for side in (LEFT, RIGHT):
                await_piece(side, step, 1, p)
                if far > 2:

                    @pl.when(step + 1 < far)
                    def _():
                        relay_piece(side, step, 1, p)

        if far > 1:
            if far == 2:
                relay_fine(step)
            else:

                @pl.when(step + 1 == far)
                def _():
                    relay_fine(step)

    take_values(1)
    blend(1)

    if far > 2:

        @pl.loop(2, far)
        def _(step):
            for p in range(parts):
                take(step, 0, p)
            take_values(step)
            blend(step)

    if far > 1:
        for p in range(parts):
            for side in (LEFT, RIGHT):
                await_piece(side, far, 0, p)

    def last(h):
        if far > 1:
            for side in (LEFT, RIGHT):

                @pl.when(gets(side, far))
                def _():
                    weights, keep = masked(h, source(side, far))
                    wb[side] = weights
                    acc[h] = acc[h] * keep

        if far > 1:
            for side in (LEFT, RIGHT):

                @pl.when(gets(side, far))
                def _():
                    fine(side, h, back=True).wait_recv()
                    acc[h] = acc[h] + mixed(wb[side], h, source(side, far))

        result = jnp.transpose(acc[h] * (1.0 / total[h])).astype(jnp.bfloat16)
        ob[:, :, lane(h)] = result.reshape(parts, rows, HEAD_DIM)
        for j in range(1, parts):
            o_exchange(h, j).start()
        out_ref[:, lane(part * heads + h)] = ob[part, :, lane(h)]

    each_head(last)

    def close_head(h):
        for j in range(1, parts):
            o_exchange(h, j).wait()
        if far > 1:
            for side in (LEFT, RIGHT):

                @pl.when(can_send(side, far))
                def _():
                    fine(side, h).wait_send()

    for i in range(3):
        for j in range(1, parts):
            exchange(j, i).wait_send()

    @pl.loop(1, far + 1)
    def _(step):
        for side in (LEFT, RIGHT):

            @pl.when(can_send(side, step))
            def _():
                for p in range(parts):
                    hop(side, step, 0, p).wait_send()

                    @pl.when((step < far) | (step == 1))
                    def _():
                        hop(side, step, 1, p).wait_send()

    each_head(close_head)


def head_groups(sizes):
    edges = [sum(sizes[:n]) for n in range(len(sizes) + 1)]
    return list(zip(edges[:-1], edges[1:]))


def helped_kernel(
    frames,
    parts,
    heads,
    columns,
    plan,
    sizes,
    lag,
    q_ref,
    k_ref,
    v_ref,
    flags_ref,
    widths_ref,
    out_ref,
    kvq,
    given,
    given_stat,
    got,
    got_stat,
    ob,
    dist,
    top,
    total,
    acc,
    local_sem,
    x_send,
    x_recv,
    n_send,
    n_recv,
    p_send,
    p_recv,
    r_send,
    r_recv,
    a_send,
    a_recv,
    s_send,
    s_recv,
    o_send,
    o_recv,
):
    frame = lax.axis_index("frame")
    part = lax.axis_index("space")
    rows = q_ref.shape[0]
    tokens = parts * rows
    inputs = (k_ref, v_ref, q_ref)
    groups = head_groups(sizes)

    def lane(head, count=1):
        return pl.ds(pl.multiple_of(head * HEAD_DIM, HEAD_DIM), count * HEAD_DIM)

    def piece(gi, p=None):
        low, high = groups[gi]
        return lane(low if p is None else p * heads + low, high - low)

    def peer(j):
        return lax.rem(part + j, parts)

    def giver(j):
        return lax.rem(part - j + parts, parts)

    def ahead(side):
        return 1 if side == RIGHT else -1

    def where(helper, side, test):
        found = None
        for at in range(1, frames - 1):
            kept = plan[side, at]
            term = None if kept is None else test(kept)
            if term is None or term is False:
                continue
            term = (helper == at) if term is True else (helper == at) & term
            found = term if found is None else found | term
        return found

    def helped(helper, side, h):
        return where(helper, side, lambda r: False if r == heads else (h >= r if r > 0 else True))

    def relayed(helper, side, h):
        return where(helper, side, lambda r: False if r == 0 else (h < r if r < heads else True))

    def when(condition, body):
        if condition is not None:
            pl.when(condition)(body)

    def has(side):
        return frame < frames - 1 if side == RIGHT else frame > 0

    def near(side):
        return frame > 0 if side == RIGHT else frame < frames - 1

    barrier = pltpu.get_barrier_semaphore()
    for j in range(1, parts):
        pl.semaphore_signal(barrier, inc=1, device_id={"space": peer(j)}, device_id_type=MESH)
    for side in (LEFT, RIGHT):

        @pl.when(has(side))
        def _():
            pl.semaphore_signal(
                barrier, inc=1, device_id={"frame": frame + ahead(side)}, device_id_type=MESH
            )

    pl.semaphore_wait(
        barrier,
        parts - 1 + jnp.where(frame > 0, 1, 0) + jnp.where(frame < frames - 1, 1, 0),
    )

    def local_copy(i):
        return pltpu.make_async_copy(
            inputs[i].at[:, lane(part * heads, heads)], kvq.at[frame, i, part], local_sem.at[i]
        )

    def exchange(j, i, gi):
        return pltpu.make_async_remote_copy(
            src_ref=inputs[i].at[:, piece(gi, peer(j))],
            dst_ref=kvq.at[frame, i, part, :, piece(gi)],
            send_sem=x_send.at[i, j - 1, gi],
            recv_sem=x_recv.at[i, j - 1, gi],
            device_id={"space": peer(j)},
            device_id_type=MESH,
        )

    def own_hop(side, i, gi, back=False):
        owner = frame - ahead(side) if back else frame
        return pltpu.make_async_remote_copy(
            src_ref=inputs[i].at[:, piece(gi, part)],
            dst_ref=kvq.at[owner, i, part, :, piece(gi)],
            send_sem=n_send.at[side, i, gi],
            recv_sem=n_recv.at[side, i, gi],
            device_id={"frame": owner if back else frame + ahead(side)},
            device_id_type=MESH,
        )

    def pass_hop(side, p, j, gi, query, back=False):
        owner = frame - ahead(side) if back else frame
        slab = kvq.at[owner, pl.ds(2, 1) if query else pl.ds(0, 2), p, :, piece(gi)]
        return pltpu.make_async_remote_copy(
            src_ref=slab,
            dst_ref=slab,
            send_sem=p_send.at[side, query, j - 1, gi],
            recv_sem=p_recv.at[side, query, j - 1, gi],
            device_id={"frame": owner if back else frame + ahead(side)},
            device_id_type=MESH,
        )

    def relay(side, i, gi, back=False):
        owner = frame - (2 if back else 1) * ahead(side)
        slab = kvq.at[owner, i, :, :, piece(gi)]
        return pltpu.make_async_remote_copy(
            src_ref=slab,
            dst_ref=slab,
            send_sem=r_send.at[side, i, gi],
            recv_sem=r_recv.at[side, i, gi],
            device_id={"frame": frame - ahead(side) if back else frame + ahead(side)},
            device_id_type=MESH,
        )

    def answer(side, h, back=False):
        to = frame - ahead(side) if back else frame + ahead(side)
        return tuple(
            pltpu.make_async_remote_copy(
                src_ref=src.at[side, h],
                dst_ref=dst.at[side, h],
                send_sem=send.at[side, h],
                recv_sem=recv.at[side, h],
                device_id={"frame": to},
                device_id_type=MESH,
            )
            for src, dst, send, recv in (
                (given, got, a_send, a_recv),
                (given_stat, got_stat, s_send, s_recv),
            )
        )

    def o_exchange(h, j):
        return pltpu.make_async_remote_copy(
            src_ref=ob.at[peer(j), :, lane(h)],
            dst_ref=out_ref.at[:, lane(part * heads + h)],
            send_sem=o_send.at[j - 1, h],
            recv_sem=o_recv.at[j - 1, h],
            device_id={"space": peer(j)},
            device_id_type=MESH,
        )

    def opposite(side):
        return LEFT if side == RIGHT else RIGHT

    def sends_query(side, gi):
        return helped(frame + ahead(side), opposite(side), groups[gi][0])

    def takes_query(side, gi):
        return helped(frame, opposite(side), groups[gi][0])

    def each_own(gi, act):
        for i in (0, 1, 2):
            for side in (LEFT, RIGHT):
                when(
                    sends_query(side, gi) if i == 2 else has(side),
                    lambda: act(own_hop(side, i, gi)),
                )

    def each_pass(gi, query, act):
        for j in range(1, parts):
            for side in (LEFT, RIGHT):
                when(
                    sends_query(side, gi) if query else has(side),
                    lambda: act(pass_hop(side, giver(j), j, gi, query)),
                )

    def each_relay(gi, act):
        for side in (LEFT, RIGHT):
            for i in (0, 1):
                when(relayed(frame, side, groups[gi][0]), lambda: act(relay(side, i, gi)))

    def begin(copy):
        copy.start()

    def drain(copy):
        copy.wait_send()

    def forward(gi):
        for query in (0, 1):
            for j in range(1, parts):
                for i in (2,) if query else (0, 1):
                    exchange(j, i, gi).wait_recv()
            each_pass(gi, query, begin)

    order = list(range(len(groups)))
    for j in range(1, parts):
        for i in range(3):
            exchange(j, i, 0).start()
    each_own(0, begin)
    if len(groups) > 1:
        each_own(order[-1], begin)
    for gi in order[1:]:
        for j in range(1, parts):
            for i in range(3):
                exchange(j, i, gi).start()
    for i in range(3):
        local_copy(i).start()

    def row_of(axis):
        at = lax.broadcasted_iota(jnp.int32, (tokens, tokens), axis).astype(jnp.float32)
        return jnp.floor((at + 0.5) * (1.0 / columns))

    dist[...] = jnp.abs(row_of(0) - row_of(1))
    top[...] = jnp.full(top.shape, NEG_FILL, jnp.float32)
    total[...] = jnp.zeros(total.shape, jnp.float32)
    acc[...] = jnp.zeros(acc.shape, jnp.float32)
    for i in range(3):
        local_copy(i).wait()

    for gi in order[:-1]:
        forward(gi)
        if gi + 1 < len(groups) - 1:
            each_own(gi + 1, begin)
    forward(order[-1])

    def await_group(gi):
        for side in (LEFT, RIGHT):
            for i in (0, 1, 2):
                when(
                    takes_query(side, gi) if i == 2 else near(side),
                    lambda: own_hop(side, i, gi, back=True).wait_recv(),
                )
            for j in range(1, parts):
                for query in (0, 1):
                    when(
                        takes_query(side, gi) if query else near(side),
                        lambda: pass_hop(side, giver(j), j, gi, query, back=True).wait_recv(),
                    )
        each_relay(gi, begin)

    def whole(f, i, h):
        return kvq[f, i, :, :, lane(h)].reshape(tokens, HEAD_DIM)

    def scores_of(h, f, g):
        gap = jnp.abs(f - g)
        reach = jnp.where(flags_ref[f, g] > 0, widths_ref[gap], -1).astype(jnp.float32)
        scores = lax.dot_general(
            whole(g, 0, h),
            whole(f, 2, h),
            (((1,), (1,)), ((), ())),
            preferred_element_type=jnp.float32,
        )
        return jnp.where(dist[...] <= reach, scores, NEG_FILL)

    def mixed(weights, h, g):
        return lax.dot_general(
            whole(g, 1, h),
            weights.astype(jnp.bfloat16),
            (((0,), (0,)), ((), ())),
            preferred_element_type=jnp.float32,
        )

    def update(h, g, between=None):
        scores = scores_of(h, frame, g)
        old_top = top[h]
        new_top = jnp.maximum(old_top, jnp.max(scores, axis=0, keepdims=True))
        weights = jnp.exp2((scores - new_top) * SCALE)
        keep = jnp.exp2((old_top - new_top) * SCALE)
        top[h] = new_top
        total[h] = total[h] * keep + jnp.sum(weights, axis=0, keepdims=True)
        if between is not None:
            between()
        acc[h] = acc[h] * keep + mixed(weights, h, g)

    def help_with(side, h):
        f, g = frame + ahead(side), frame - ahead(side)
        scores = scores_of(h, f, g)
        peak = jnp.max(scores, axis=0, keepdims=True)
        weights = jnp.exp2((scores - peak) * SCALE)
        given_stat[side, h, 0:1] = peak
        given_stat[side, h, 1:2] = jnp.sum(weights, axis=0, keepdims=True)
        given[side, h] = mixed(weights, h, g).astype(jnp.bfloat16)
        for copy in answer(side, h):
            copy.start()

    def compute(h):
        for gi, (low, _high) in enumerate(groups):

            @pl.when(h == low)
            def _():
                await_group(gi)

        for side in (LEFT, RIGHT):
            when(helped(frame, side, h), lambda: help_with(side, h))

        update(h, frame)
        for side in (LEFT, RIGHT):

            @pl.when(near(side))
            def _():
                update(h, frame - ahead(side))

    def await_relay(side, i, h):
        for gi, (low, _high) in enumerate(groups):
            incoming = relayed(frame - ahead(side), side, low)
            if incoming is not None:

                @pl.when(h == low)
                def _():
                    relay(side, i, gi, back=True).wait_recv()

    def take_relay(side, h):
        await_relay(side, 0, h)
        update(h, frame - 2 * ahead(side), lambda: await_relay(side, 1, h))

    def take_answer(side, h):
        for copy in answer(side, h, back=True):
            copy.wait_recv()
        peak = got_stat[side, h, 0:1]
        new_top = jnp.maximum(top[h], peak)
        keep = jnp.exp2((top[h] - new_top) * SCALE)
        add = jnp.exp2((peak - new_top) * SCALE)
        total[h] = total[h] * keep + got_stat[side, h, 1:2] * add
        acc[h] = acc[h] * keep + got[side, h].astype(jnp.float32) * add

    def finish(h):
        for side in (LEFT, RIGHT):
            helper = frame - ahead(side)
            when(relayed(helper, side, h), lambda: take_relay(side, h))
            when(helped(helper, side, h), lambda: take_answer(side, h))

        result = jnp.transpose(acc[h] * (1.0 / total[h])).astype(jnp.bfloat16)
        ob[:, :, lane(h)] = result.reshape(parts, rows, HEAD_DIM)
        for j in range(1, parts):
            o_exchange(h, j).start()
        out_ref[:, lane(part * heads + h)] = ob[part, :, lane(h)]

    @pl.loop(0, heads + lag)
    def _(step):
        @pl.when(step < heads)
        def _():
            compute(step)

        @pl.when(step >= lag)
        def _():
            finish(step - lag)

    for gi in order:
        for j in range(1, parts):
            for i in range(3):
                exchange(j, i, gi).wait_send()
        each_own(gi, drain)
        for query in (0, 1):
            each_pass(gi, query, drain)
        each_relay(gi, drain)

    @pl.loop(0, heads)
    def _(h):
        for side in (LEFT, RIGHT):

            def drained():
                for copy in answer(side, h):
                    copy.wait_send()

            when(helped(frame, side, h), drained)

        for j in range(1, parts):
            o_exchange(h, j).wait()


def choose_kernel(frames, flags_in, widths_in, index_ref, flags_ref, widths_ref):
    right = flags_in[frames - 2, 0] > 0
    left = flags_in[1, frames - 1] > 0
    index_ref[0] = jnp.where(left, jnp.where(right, 0, 2), 1)
    for f in range(frames):
        widths_ref[f] = widths_in[f]
        for g in range(frames):
            flags_ref[f, g] = flags_in[f, g]


def shards(frames, parts, queries, keys, values, flags, widths):
    shape = queries.shape
    columns, features = shape[2], shape[3]
    rows = shape[1] * columns
    heads = features // HEAD_DIM // parts
    tokens = rows * parts
    far = frames - 2
    flat = [a.reshape(rows, features) for a in (queries, keys, values)]
    any_spec = pl.BlockSpec(memory_space=pl.ANY)
    others = max(parts - 1, 1)
    dma = pltpu.SemaphoreType.DMA
    vmem = pltpu.VMEM
    width = heads * HEAD_DIM
    tables = [pltpu.SMEM(flags.shape, jnp.int32), pltpu.SMEM(widths.shape, jnp.int32), dma((2,))]
    scalar_spec = pl.BlockSpec(memory_space=pltpu.SMEM)
    common = dict(
        out_shape=vmem((rows, features), jnp.bfloat16),
        out_specs=pl.BlockSpec(memory_space=vmem),
    )

    def full(*operands):
        return pl.pallas_call(
            functools.partial(kernel, frames, parts, heads, columns),
            scratch_shapes=[
                vmem((frames, 2, parts, rows, width), jnp.bfloat16),
                vmem((parts, rows, width), jnp.bfloat16),
                vmem((parts, rows, width), jnp.bfloat16),
                vmem((tokens, tokens), jnp.float32),
                vmem((2, tokens, tokens), jnp.bfloat16),
                vmem((heads, 1, tokens), jnp.float32),
                vmem((heads, 1, tokens), jnp.float32),
                vmem((heads, HEAD_DIM, tokens), jnp.float32),
                dma((3,)),
                dma((3, others)),
                dma((3, others)),
                dma((2, far, 2, parts)),
                dma((2, far, 2, parts)),
                dma((2, heads)),
                dma((2, heads)),
                dma((others, heads)),
                dma((others, heads)),
            ]
            + tables,
            compiler_params=pltpu.CompilerParams(collective_id=0, has_side_effects=True),
            in_specs=[any_spec] * 5,
            name="full",
            **common,
        )(*operands)

    def helped(collective_id, plan, sizes, lag):
        pieces = len(sizes)

        def call(*operands):
            return pl.pallas_call(
                functools.partial(helped_kernel, frames, parts, heads, columns, plan, sizes, lag),
                scratch_shapes=[
                    vmem((frames, 3, parts, rows, width), jnp.bfloat16),
                    vmem((2, heads, HEAD_DIM, tokens), jnp.bfloat16),
                    vmem((2, heads, 8, tokens), jnp.float32),
                    vmem((2, heads, HEAD_DIM, tokens), jnp.bfloat16),
                    vmem((2, heads, 8, tokens), jnp.float32),
                    vmem((parts, rows, width), jnp.bfloat16),
                    vmem((tokens, tokens), jnp.float32),
                    vmem((heads, 1, tokens), jnp.float32),
                    vmem((heads, 1, tokens), jnp.float32),
                    vmem((heads, HEAD_DIM, tokens), jnp.float32),
                    dma((3,)),
                    dma((3, others, pieces)),
                    dma((3, others, pieces)),
                    dma((2, 3, pieces)),
                    dma((2, 3, pieces)),
                    dma((2, 2, others, pieces)),
                    dma((2, 2, others, pieces)),
                    dma((2, 2, pieces)),
                    dma((2, 2, pieces)),
                    dma((2, heads)),
                    dma((2, heads)),
                    dma((2, heads)),
                    dma((2, heads)),
                    dma((others, heads)),
                    dma((others, heads)),
                ],
                in_specs=[any_spec] * 3 + [scalar_spec] * 2,
                compiler_params=pltpu.CompilerParams(
                    collective_id=collective_id, has_side_effects=True
                ),
                name=f"helped{collective_id}",
                **common,
            )(*operands)

        return call

    if far == 2:
        index, *chosen = pl.pallas_call(
            functools.partial(choose_kernel, frames),
            out_shape=[
                pltpu.SMEM((1,), jnp.int32),
                pltpu.SMEM(flags.shape, jnp.int32),
                pltpu.SMEM(widths.shape, jnp.int32),
            ],
            in_specs=[scalar_spec] * 2,
            out_specs=[scalar_spec] * 3,
            name="choose",
        )(flags, widths)
        inner = [(side, at) for side in (LEFT, RIGHT) for at in range(1, frames - 1)]
        far_left, far_right = (LEFT, frames - 2), (RIGHT, 1)
        half = heads // 2
        front = min(1, heads - 1)
        coarse = [n for n in (half, heads - half - 1, 1) if n]
        small = [1] * heads
        whole = {key: heads if key in (far_left, far_right) else 0 for key in inner}
        branches = [helped(0, whole, coarse, heads)] + [
            helped(n, {key: None if key == gone else front for key in inner}, small, min(2, heads))
            for n, gone in ((1, far_left), (2, far_right))
        ]
        out = lax.switch(index[0], branches, *flat, *chosen)
    else:
        out = full(*flat, flags, widths)
    return out.reshape(shape)


def solution(mesh):
    spec = P(("group", "frame"), "space", None, "head")
    return jax.shard_map(
        functools.partial(shards, mesh.shape["frame"], mesh.shape["space"]),
        mesh=mesh,
        in_specs=(spec, spec, spec, P(), P()),
        out_specs=spec,
        check_vma=False,
    )
```

```python
import functools
import math

import jax
import jax.numpy as jnp
from jax import lax
from jax.experimental import pallas as pl
from jax.experimental.pallas import tpu as pltpu
from jax.sharding import PartitionSpec as P

HEAD_DIM = 128
NEG_FILL = -1e30
SCALE = math.log2(math.e) / HEAD_DIM**0.5
MESH = pl.DeviceIdType.MESH
LEFT, RIGHT = 0, 1


def kernel(
    frames,
    parts,
    heads,
    columns,
    q_ref,
    k_ref,
    v_ref,
    flags_in,
    widths_in,
    out_ref,
    kv,
    qb,
    ob,
    dist,
    wb,
    top,
    total,
    acc,
    local_sem,
    x_send,
    x_recv,
    z_send,
    z_recv,
    f_send,
    f_recv,
    o_send,
    o_recv,
    flags_ref,
    widths_ref,
    table_sem,
):
    frame = lax.axis_index("frame")
    part = lax.axis_index("space")
    rows = q_ref.shape[0]
    tokens = parts * rows
    width = heads * HEAD_DIM
    far = frames - 2
    inputs = (k_ref, v_ref, q_ref)

    def lane(head):
        return pl.ds(pl.multiple_of(head * HEAD_DIM, HEAD_DIM), HEAD_DIM)

    def span(p):
        return pl.ds(pl.multiple_of(p * width, HEAD_DIM), width)

    def peer(j):
        return lax.rem(part + j, parts)

    def home(i):
        return qb.at[part] if i == 2 else kv.at[frame, i, part]

    barrier = pltpu.get_barrier_semaphore()
    for j in range(1, parts):
        pl.semaphore_signal(barrier, inc=1, device_id={"space": peer(j)}, device_id_type=MESH)

    @pl.when(frame > 0)
    def _():
        pl.semaphore_signal(barrier, inc=1, device_id={"frame": frame - 1}, device_id_type=MESH)

    @pl.when(frame < frames - 1)
    def _():
        pl.semaphore_signal(barrier, inc=1, device_id={"frame": frame + 1}, device_id_type=MESH)

    def local_copy(i):
        return pltpu.make_async_copy(inputs[i].at[:, span(part)], home(i), local_sem.at[i])

    def exchange(j, i):
        return pltpu.make_async_remote_copy(
            src_ref=inputs[i].at[:, span(peer(j))],
            dst_ref=home(i),
            send_sem=x_send.at[i, j - 1],
            recv_sem=x_recv.at[i, j - 1],
            device_id={"space": peer(j)},
            device_id_type=MESH,
        )

    def o_exchange(h, j):
        return pltpu.make_async_remote_copy(
            src_ref=ob.at[peer(j), :, lane(h)],
            dst_ref=out_ref.at[:, lane(part * heads + h)],
            send_sem=o_send.at[j - 1, h],
            recv_sem=o_recv.at[j - 1, h],
            device_id={"space": peer(j)},
            device_id_type=MESH,
        )

    def towards(side):
        return 1 if side == RIGHT else -1

    def hop(side, step, i, p, src=None, back=False):
        ahead = towards(side)
        owner = frame - ahead * (step if back else step - 1)
        block = kv.at[owner, i, p]
        return pltpu.make_async_remote_copy(
            src_ref=block if src is None else src,
            dst_ref=block,
            send_sem=z_send.at[side, step - 1, i, p],
            recv_sem=z_recv.at[side, step - 1, i, p],
            device_id={"frame": frame - ahead if back else frame + ahead},
            device_id_type=MESH,
        )

    def fine(side, h, back=False):
        ahead = towards(side)
        owner = frame - ahead * (far if back else far - 1)
        block = kv.at[owner, 1, :, :, lane(h)]
        return pltpu.make_async_remote_copy(
            src_ref=block,
            dst_ref=block,
            send_sem=f_send.at[side, h],
            recv_sem=f_recv.at[side, h],
            device_id={"frame": frame - ahead if back else frame + ahead},
            device_id_type=MESH,
        )

    def can_send(side, step):
        if side == RIGHT:
            return (frame < frames - 1) & (frame - (step - 1) >= 0)
        return (frame > 0) & (frame + (step - 1) <= frames - 1)

    def gets(side, step):
        if side == RIGHT:
            return frame - step >= 0
        return frame + step <= frames - 1

    def source(side, step):
        return frame - step if side == RIGHT else frame + step

    def each_head(body):
        @pl.loop(0, heads)
        def _(h):
            body(h)

    pl.semaphore_wait(
        barrier,
        parts - 1 + jnp.where(frame > 0, 1, 0) + jnp.where(frame < frames - 1, 1, 0),
    )

    for i in (0, 1):
        for j in range(1, parts):
            exchange(j, i).start()
        for side in (LEFT, RIGHT):

            @pl.when(can_send(side, 1))
            def _():
                hop(side, 1, i, part, inputs[i].at[:, span(part)]).start()

    tables = (
        pltpu.make_async_copy(flags_in, flags_ref, table_sem.at[0]),
        pltpu.make_async_copy(widths_in, widths_ref, table_sem.at[1]),
    )
    for copy in tables:
        copy.start()
    for i in range(3):
        local_copy(i).start()
    for j in range(1, parts):
        exchange(j, 2).start()

    def row_of(axis):
        at = lax.broadcasted_iota(jnp.int32, (tokens, tokens), axis).astype(jnp.float32)
        return jnp.floor((at + 0.5) * (1.0 / columns))

    dist[...] = jnp.abs(row_of(0) - row_of(1))
    top[...] = jnp.full(top.shape, NEG_FILL, jnp.float32)
    total[...] = jnp.zeros(total.shape, jnp.float32)
    acc[...] = jnp.zeros(acc.shape, jnp.float32)

    def await_piece(side, step, i, p):
        @pl.when(gets(side, step))
        def _():
            hop(side, step, i, p, back=True).wait_recv()

    def relay_piece(side, step, i, p):
        @pl.when(gets(side, step) & can_send(side, step + 1))
        def _():
            hop(side, step + 1, i, p).start()

    def relay_fine(step):
        for side in (LEFT, RIGHT):

            @pl.when(gets(side, step) & can_send(side, step + 1))
            def _():
                each_head(lambda h: fine(side, h).start())

    def pass_piece(i):
        for j in range(1, parts):
            p = lax.rem(part - j + parts, parts)
            exchange(j, i).wait_recv()
            for side in (LEFT, RIGHT):

                @pl.when(can_send(side, 1))
                def _():
                    hop(side, 1, i, p).start()

    def take(step, i, p):
        for side in (LEFT, RIGHT):
            await_piece(side, step, i, p)
            if far > 1:
                relay_piece(side, step, i, p)

    pass_piece(0)
    take(1, 0, part)
    pass_piece(1)
    for copy in tables:
        copy.wait()

    def masked(h, g):
        gap = jnp.abs(frame - g)
        reach = jnp.where(flags_ref[frame, g] > 0, widths_ref[gap], -1).astype(jnp.float32)
        keys = kv[g, 0, :, :, lane(h)].reshape(tokens, HEAD_DIM)
        queries = qb[:, :, lane(h)].reshape(tokens, HEAD_DIM)
        scores = lax.dot_general(
            keys, queries, (((1,), (1,)), ((), ())), preferred_element_type=jnp.float32
        )
        scores = jnp.where(dist[...] <= reach, scores, NEG_FILL)
        old_top = top[h]
        new_top = jnp.maximum(old_top, jnp.max(scores, axis=0, keepdims=True))
        weights = jnp.exp2((scores - new_top) * SCALE)
        keep = jnp.exp2((old_top - new_top) * SCALE)
        top[h] = new_top
        total[h] = total[h] * keep + jnp.sum(weights, axis=0, keepdims=True)
        return weights.astype(jnp.bfloat16), keep

    def mixed(weights, h, g):
        vals = kv[g, 1, :, :, lane(h)].reshape(tokens, HEAD_DIM)
        return lax.dot_general(
            vals, weights, (((0,), (0,)), ((), ())), preferred_element_type=jnp.float32
        )

    def update(h, g):
        weights, keep = masked(h, g)
        acc[h] = acc[h] * keep + mixed(weights, h, g)

    def blend(step):
        def body(h):
            for side in (LEFT, RIGHT):

                @pl.when(gets(side, step))
                def _():
                    update(h, source(side, step))

        each_head(body)

    for j in range(1, parts):
        take(1, 0, peer(j))
    for i in range(3):
        local_copy(i).wait()
    for j in range(1, parts):
        exchange(j, 2).wait_recv()
    each_head(lambda h: update(h, frame))

    def take_values(step):
        for p in range(parts):
            for side in (LEFT, RIGHT):
                await_piece(side, step, 1, p)
                if far > 2:

                    @pl.when(step + 1 < far)
                    def _():
                        relay_piece(side, step, 1, p)

        if far > 1:
            if far == 2:
                relay_fine(step)
            else:

                @pl.when(step + 1 == far)
                def _():
                    relay_fine(step)

    take_values(1)
    blend(1)

    if far > 2:

        @pl.loop(2, far)
        def _(step):
            for p in range(parts):
                take(step, 0, p)
            take_values(step)
            blend(step)

    if far > 1:
        for p in range(parts):
            for side in (LEFT, RIGHT):
                await_piece(side, far, 0, p)

    def last(h):
        if far > 1:
            for side in (LEFT, RIGHT):

                @pl.when(gets(side, far))
                def _():
                    weights, keep = masked(h, source(side, far))
                    wb[side] = weights
                    acc[h] = acc[h] * keep

        if far > 1:
            for side in (LEFT, RIGHT):

                @pl.when(gets(side, far))
                def _():
                    fine(side, h, back=True).wait_recv()
                    acc[h] = acc[h] + mixed(wb[side], h, source(side, far))

        result = jnp.transpose(acc[h] * (1.0 / total[h])).astype(jnp.bfloat16)
        ob[:, :, lane(h)] = result.reshape(parts, rows, HEAD_DIM)
        for j in range(1, parts):
            o_exchange(h, j).start()
        out_ref[:, lane(part * heads + h)] = ob[part, :, lane(h)]

    each_head(last)

    def close_head(h):
        for j in range(1, parts):
            o_exchange(h, j).wait()
        if far > 1:
            for side in (LEFT, RIGHT):

                @pl.when(can_send(side, far))
                def _():
                    fine(side, h).wait_send()

    for i in range(3):
        for j in range(1, parts):
            exchange(j, i).wait_send()

    @pl.loop(1, far + 1)
    def _(step):
        for side in (LEFT, RIGHT):

            @pl.when(can_send(side, step))
            def _():
                for p in range(parts):
                    hop(side, step, 0, p).wait_send()

                    @pl.when((step < far) | (step == 1))
                    def _():
                        hop(side, step, 1, p).wait_send()

    each_head(close_head)


def head_groups(sizes):
    edges = [sum(sizes[:n]) for n in range(len(sizes) + 1)]
    return list(zip(edges[:-1], edges[1:]))


def helped_kernel(
    frames,
    parts,
    heads,
    columns,
    plan,
    sizes,
    lag,
    q_ref,
    k_ref,
    v_ref,
    flags_ref,
    widths_ref,
    out_ref,
    kvq,
    given,
    given_stat,
    got,
    got_stat,
    mine,
    mine_stat,
    held,
    held_stat,
    ob,
    dist,
    top,
    total,
    acc,
    local_sem,
    x_send,
    x_recv,
    n_send,
    n_recv,
    p_send,
    p_recv,
    r_send,
    r_recv,
    a_send,
    a_recv,
    s_send,
    s_recv,
    m_send,
    m_recv,
    o_send,
    o_recv,
):
    frame = lax.axis_index("frame")
    part = lax.axis_index("space")
    rows = q_ref.shape[0]
    tokens = parts * rows
    inputs = (k_ref, v_ref, q_ref)
    groups = head_groups(sizes)

    def lane(head, count=1):
        return pl.ds(pl.multiple_of(head * HEAD_DIM, HEAD_DIM), count * HEAD_DIM)

    def piece(gi, p=None):
        low, high = groups[gi]
        return lane(low if p is None else p * heads + low, high - low)

    def peer(j):
        return lax.rem(part + j, parts)

    def giver(j):
        return lax.rem(part - j + parts, parts)

    def ahead(side):
        return 1 if side == RIGHT else -1

    def where(helper, side, test):
        found = None
        for at in range(1, frames - 1):
            kept = plan[side, at]
            term = None if kept is None else test(kept)
            if term is None or term is False:
                continue
            term = (helper == at) if term is True else (helper == at) & term
            found = term if found is None else found | term
        return found

    def helped(helper, side, h):
        return where(helper, side, lambda r: False if r == heads else (h >= r if r > 0 else True))

    def relayed(helper, side, h):
        return where(helper, side, lambda r: False if r == 0 else (h < r if r < heads else True))

    def when(condition, body):
        if condition is not None:
            pl.when(condition)(body)

    def has(side):
        return frame < frames - 1 if side == RIGHT else frame > 0

    def near(side):
        return frame > 0 if side == RIGHT else frame < frames - 1

    barrier = pltpu.get_barrier_semaphore()
    for j in range(1, parts):
        pl.semaphore_signal(barrier, inc=1, device_id={"space": peer(j)}, device_id_type=MESH)
    for side in (LEFT, RIGHT):

        @pl.when(has(side))
        def _():
            for p in range(parts):
                pl.semaphore_signal(
                    barrier,
                    inc=1,
                    device_id={"frame": frame + ahead(side), "space": p},
                    device_id_type=MESH,
                )

    pl.semaphore_wait(
        barrier,
        parts - 1 + jnp.where(frame > 0, parts, 0) + jnp.where(frame < frames - 1, parts, 0),
    )

    def local_copy(i):
        return pltpu.make_async_copy(
            inputs[i].at[:, lane(part * heads, heads)], kvq.at[frame, i, part], local_sem.at[i]
        )

    def exchange(j, i, gi):
        return pltpu.make_async_remote_copy(
            src_ref=inputs[i].at[:, piece(gi, peer(j))],
            dst_ref=kvq.at[frame, i, part, :, piece(gi)],
            send_sem=x_send.at[i, j - 1, gi],
            recv_sem=x_recv.at[i, j - 1, gi],
            device_id={"space": peer(j)},
            device_id_type=MESH,
        )

    def own_hop(side, i, gi, back=False):
        owner = frame - ahead(side) if back else frame
        return pltpu.make_async_remote_copy(
            src_ref=inputs[i].at[:, piece(gi, part)],
            dst_ref=kvq.at[owner, i, part, :, piece(gi)],
            send_sem=n_send.at[side, i, gi],
            recv_sem=n_recv.at[side, i, gi],
            device_id={"frame": owner if back else frame + ahead(side)},
            device_id_type=MESH,
        )

    def slab_hop(side, p, slot, gi, query, back=False):
        owner = frame - ahead(side) if back else frame
        slab = kvq.at[owner, pl.ds(0, 3 if query else 2), p, :, piece(gi)]
        return pltpu.make_async_remote_copy(
            src_ref=slab,
            dst_ref=slab,
            send_sem=p_send.at[side, slot, gi],
            recv_sem=p_recv.at[side, slot, gi],
            device_id={"frame": owner if back else frame + ahead(side)},
            device_id_type=MESH,
        )

    def relay(side, i, gi, back=False):
        owner = frame - (2 if back else 1) * ahead(side)
        slab = kvq.at[owner, pl.ds(0, 2) if i is None else pl.ds(i, 1), :, :, piece(gi)]
        return pltpu.make_async_remote_copy(
            src_ref=slab,
            dst_ref=slab,
            send_sem=r_send.at[side, i or 0, gi],
            recv_sem=r_recv.at[side, i or 0, gi],
            device_id={"frame": frame - ahead(side) if back else frame + ahead(side)},
            device_id_type=MESH,
        )

    def answer(side, h, p, back=False):
        to = frame - ahead(side) if back else frame + ahead(side)
        slot = p if back else part
        return tuple(
            pltpu.make_async_remote_copy(
                src_ref=src.at[side, h, p],
                dst_ref=dst.at[side, h, slot],
                send_sem=send.at[side, h, p],
                recv_sem=recv.at[side, h, slot],
                device_id={"frame": to, "space": p},
                device_id_type=MESH,
            )
            for src, dst, send, recv in (
                (given, got, a_send, a_recv),
                (given_stat, got_stat, s_send, s_recv),
            )
        )

    def share(h, j, back=False):
        slot = giver(j) if back else part
        to = peer(j)
        return tuple(
            pltpu.make_async_remote_copy(
                src_ref=src.at[h, to],
                dst_ref=dst.at[h, slot],
                send_sem=m_send.at[n, h, j - 1],
                recv_sem=m_recv.at[n, h, j - 1],
                device_id={"space": to},
                device_id_type=MESH,
            )
            for n, (src, dst) in enumerate(((mine, held), (mine_stat, held_stat)))
        )

    def o_exchange(h, j):
        return pltpu.make_async_remote_copy(
            src_ref=ob.at[peer(j), :, lane(h)],
            dst_ref=out_ref.at[:, lane(part * heads + h)],
            send_sem=o_send.at[j - 1, h],
            recv_sem=o_recv.at[j - 1, h],
            device_id={"space": peer(j)},
            device_id_type=MESH,
        )

    def opposite(side):
        return LEFT if side == RIGHT else RIGHT

    def sends_query(side, gi):
        return helped(frame + ahead(side), opposite(side), groups[gi][0])

    def takes_query(side, gi):
        return helped(frame, opposite(side), groups[gi][0])

    def direct(gi):
        return gi in (0, len(groups) - 1)

    def each_side(side, gi, query, plain, asked):
        if query is None:
            pl.when(plain)(lambda: asked(False))
        else:
            pl.when(query)(lambda: asked(True))
            pl.when(plain & jnp.logical_not(query))(lambda: asked(False))

    def each_own(gi, act):
        for side in (LEFT, RIGHT):
            query = sends_query(side, gi)
            if direct(gi):
                for i in (0, 1, 2):
                    when(query if i == 2 else has(side), lambda: act(own_hop(side, i, gi)))
            else:
                each_side(
                    side, gi, query, has(side), lambda q: act(slab_hop(side, part, 0, gi, q))
                )

    def each_pass(gi, act):
        for j in range(1, parts):
            for side in (LEFT, RIGHT):
                each_side(
                    side,
                    gi,
                    sends_query(side, gi),
                    has(side),
                    lambda q: act(slab_hop(side, giver(j), j, gi, q)),
                )

    def relay_steps(gi):
        return (0, 1) if gi == len(groups) - 1 else (None,)

    def each_relay(gi, act):
        for side in (LEFT, RIGHT):
            for i in relay_steps(gi):
                when(relayed(frame, side, groups[gi][0]), lambda: act(relay(side, i, gi)))

    def begin(copy):
        copy.start()

    def drain(copy):
        copy.wait_send()

    def forward(gi):
        for i in range(3):
            for j in range(1, parts):
                exchange(j, i, gi).wait_recv()
            if i == 0:
                continue
            for j in range(1, parts):
                for side in (LEFT, RIGHT):
                    query = sends_query(side, gi)
                    ready = query
                    if i == 1:
                        ready = has(side)
                        if query is not None:
                            ready = ready & jnp.logical_not(query)
                    when(ready, lambda: slab_hop(side, giver(j), j, gi, i == 2).start())

    order = list(range(len(groups)))
    for j in range(1, parts):
        for i in range(3):
            exchange(j, i, 0).start()
    each_own(0, begin)
    if len(groups) > 1:
        each_own(order[-1], begin)
    for gi in order[1:]:
        for j in range(1, parts):
            for i in range(3):
                exchange(j, i, gi).start()
    for i in range(3):
        local_copy(i).start()

    def row_of(axis):
        at = lax.broadcasted_iota(jnp.int32, (tokens, tokens), axis).astype(jnp.float32)
        return jnp.floor((at + 0.5) * (1.0 / columns))

    dist[...] = jnp.abs(row_of(0) - row_of(1))
    top[...] = jnp.full(top.shape, NEG_FILL, jnp.float32)
    total[...] = jnp.zeros(total.shape, jnp.float32)
    acc[...] = jnp.zeros(acc.shape, jnp.float32)
    for i in range(3):
        local_copy(i).wait()

    for gi in order[:-1]:
        forward(gi)
        if gi + 1 < len(groups) - 1:
            each_own(gi + 1, begin)
    forward(order[-1])

    def await_group(gi):
        for side in (LEFT, RIGHT):
            query = takes_query(side, gi)
            if direct(gi):
                for i in (0, 1, 2):
                    when(
                        query if i == 2 else near(side),
                        lambda: own_hop(side, i, gi, back=True).wait_recv(),
                    )
            for slot in range(1 if direct(gi) else 0, parts):
                p = giver(slot) if slot else part
                each_side(
                    side,
                    gi,
                    query,
                    near(side),
                    lambda q: slab_hop(side, p, slot, gi, q, back=True).wait_recv(),
                )
        each_relay(gi, begin)

    def whole(f, i, h):
        return kvq[f, i, :, :, lane(h)].reshape(tokens, HEAD_DIM)

    def scores_of(h, f, g):
        gap = jnp.abs(f - g)
        reach = jnp.where(flags_ref[f, g] > 0, widths_ref[gap], -1).astype(jnp.float32)
        scores = lax.dot_general(
            whole(g, 0, h),
            whole(f, 2, h),
            (((1,), (1,)), ((), ())),
            preferred_element_type=jnp.float32,
        )
        return jnp.where(dist[...] <= reach, scores, NEG_FILL)

    def mixed(weights, h, g):
        return lax.dot_general(
            whole(g, 1, h),
            weights.astype(jnp.bfloat16),
            (((0,), (0,)), ((), ())),
            preferred_element_type=jnp.float32,
        )

    def update(h, g, between=None):
        scores = scores_of(h, frame, g)
        old_top = top[h]
        new_top = jnp.maximum(old_top, jnp.max(scores, axis=0, keepdims=True))
        weights = jnp.exp2((scores - new_top) * SCALE)
        keep = jnp.exp2((old_top - new_top) * SCALE)
        top[h] = new_top
        total[h] = total[h] * keep + jnp.sum(weights, axis=0, keepdims=True)
        if between is not None:
            between()
        acc[h] = acc[h] * keep + mixed(weights, h, g)

    def split(values, stats, result, peak, mass):
        turned = jnp.transpose(result).astype(jnp.bfloat16)
        for p in range(parts):
            cut = slice(p * rows, (p + 1) * rows)
            values[p] = turned[cut]
            stats[p, 0:1] = peak[:, cut]
            stats[p, 1:2] = mass[:, cut]

    def help_with(side, h):
        f, g = frame + ahead(side), frame - ahead(side)
        scores = scores_of(h, f, g)
        peak = jnp.max(scores, axis=0, keepdims=True)
        weights = jnp.exp2((scores - peak) * SCALE)
        split(
            given.at[side, h],
            given_stat.at[side, h],
            mixed(weights, h, g),
            peak,
            jnp.sum(weights, axis=0, keepdims=True),
        )
        for p in range(parts):
            for copy in answer(side, h, p):
                copy.start()

    def compute(h):
        for gi, (low, _high) in enumerate(groups):

            @pl.when(h == low)
            def _():
                await_group(gi)

        for side in (LEFT, RIGHT):
            when(helped(frame, side, h), lambda: help_with(side, h))

        update(h, frame)
        for side in (LEFT, RIGHT):

            @pl.when(near(side))
            def _():
                update(h, frame - ahead(side))

        def share_all():
            split(mine.at[h], mine_stat.at[h], acc[h], top[h], total[h])
            for j in range(1, parts):
                for copy in share(h, j):
                    copy.start()

        for side in (LEFT, RIGHT):
            when(helped(frame - ahead(side), side, h), share_all)

    def await_relay(side, i, h):
        for gi, (low, _high) in enumerate(groups):
            steps = relay_steps(gi)
            if relayed(frame - ahead(side), side, low) is None or (i and i not in steps):
                continue

            @pl.when(h == low)
            def _():
                relay(side, i if i in steps else None, gi, back=True).wait_recv()

    def take_relay(side, h):
        await_relay(side, 0, h)
        update(h, frame - 2 * ahead(side), lambda: await_relay(side, 1, h))

    def merge(h, p, values, stats, far_values, far_stats):
        peak, far_peak = stats[0:1], far_stats[0:1]
        new_top = jnp.maximum(peak, far_peak)
        keep = jnp.exp2((peak - new_top) * SCALE)
        add = jnp.exp2((far_peak - new_top) * SCALE)
        mass = 1.0 / (stats[1:2] * keep + far_stats[1:2] * add)
        share_of = jnp.concatenate([keep * mass, add * mass] * 4, axis=0)
        column = jnp.transpose(share_of)
        result = values[...].astype(jnp.float32) * column[:, 0:1]
        result = result + far_values[...].astype(jnp.float32) * column[:, 1:2]
        out_ref[:, lane(p * heads + h)] = result.astype(jnp.bfloat16)

    def take_answer(side, h):
        for j in range(parts):
            p = giver(j) if j else part
            if j:
                for copy in share(h, j, back=True):
                    copy.wait_recv()
            for copy in answer(side, h, p, back=True):
                copy.wait_recv()
            kept, kept_stat = (held, held_stat) if j else (mine, mine_stat)
            merge(h, p, kept.at[h, p], kept_stat.at[h, p], got.at[side, h, p], got_stat.at[side, h, p])

    def elsewhere(h):
        answered = None
        for side in (LEFT, RIGHT):
            term = helped(frame - ahead(side), side, h)
            if term is not None:
                answered = term if answered is None else answered | term
        return answered

    def unless(condition, body):
        if condition is None:
            body()
        else:
            pl.when(jnp.logical_not(condition))(body)

    def finish(h):
        for side in (LEFT, RIGHT):
            helper = frame - ahead(side)
            when(relayed(helper, side, h), lambda: take_relay(side, h))
            when(helped(helper, side, h), lambda: take_answer(side, h))

        def write():
            result = jnp.transpose(acc[h] * (1.0 / total[h])).astype(jnp.bfloat16)
            ob[:, :, lane(h)] = result.reshape(parts, rows, HEAD_DIM)
            for j in range(1, parts):
                o_exchange(h, j).start()
            out_ref[:, lane(part * heads + h)] = ob[part, :, lane(h)]

        unless(elsewhere(h), write)

    @pl.loop(0, heads + lag)
    def _(step):
        @pl.when(step < heads)
        def _():
            compute(step)

        @pl.when(step >= lag)
        def _():
            finish(step - lag)

    for gi in order:
        for j in range(1, parts):
            for i in range(3):
                exchange(j, i, gi).wait_send()
        each_own(gi, drain)
        each_pass(gi, drain)
        each_relay(gi, drain)

    @pl.loop(0, heads)
    def _(h):
        for side in (LEFT, RIGHT):

            def drained():
                for p in range(parts):
                    for copy in answer(side, h, p):
                        copy.wait_send()

            def shared():
                for j in range(1, parts):
                    for copy in share(h, j):
                        copy.wait_send()

            when(helped(frame, side, h), drained)
            when(helped(frame - ahead(side), side, h), shared)

        def written():
            for j in range(1, parts):
                o_exchange(h, j).wait()

        unless(elsewhere(h), written)


def choose_kernel(frames, flags_in, widths_in, index_ref, flags_ref, widths_ref):
    right = flags_in[frames - 2, 0] > 0
    left = flags_in[1, frames - 1] > 0
    index_ref[0] = jnp.where(left, jnp.where(right, 0, 2), 1)
    for f in range(frames):
        widths_ref[f] = widths_in[f]
        for g in range(frames):
            flags_ref[f, g] = flags_in[f, g]


def shards(frames, parts, queries, keys, values, flags, widths):
    shape = queries.shape
    columns, features = shape[2], shape[3]
    rows = shape[1] * columns
    heads = features // HEAD_DIM // parts
    tokens = rows * parts
    far = frames - 2
    flat = [a.reshape(rows, features) for a in (queries, keys, values)]
    any_spec = pl.BlockSpec(memory_space=pl.ANY)
    others = max(parts - 1, 1)
    dma = pltpu.SemaphoreType.DMA
    vmem = pltpu.VMEM
    width = heads * HEAD_DIM
    tables = [pltpu.SMEM(flags.shape, jnp.int32), pltpu.SMEM(widths.shape, jnp.int32), dma((2,))]
    scalar_spec = pl.BlockSpec(memory_space=pltpu.SMEM)
    common = dict(
        out_shape=vmem((rows, features), jnp.bfloat16),
        out_specs=pl.BlockSpec(memory_space=vmem),
    )

    def full(*operands):
        return pl.pallas_call(
            functools.partial(kernel, frames, parts, heads, columns),
            scratch_shapes=[
                vmem((frames, 2, parts, rows, width), jnp.bfloat16),
                vmem((parts, rows, width), jnp.bfloat16),
                vmem((parts, rows, width), jnp.bfloat16),
                vmem((tokens, tokens), jnp.float32),
                vmem((2, tokens, tokens), jnp.bfloat16),
                vmem((heads, 1, tokens), jnp.float32),
                vmem((heads, 1, tokens), jnp.float32),
                vmem((heads, HEAD_DIM, tokens), jnp.float32),
                dma((3,)),
                dma((3, others)),
                dma((3, others)),
                dma((2, far, 2, parts)),
                dma((2, far, 2, parts)),
                dma((2, heads)),
                dma((2, heads)),
                dma((others, heads)),
                dma((others, heads)),
            ]
            + tables,
            compiler_params=pltpu.CompilerParams(collective_id=0, has_side_effects=True),
            in_specs=[any_spec] * 5,
            name="full",
            **common,
        )(*operands)

    def helped(collective_id, plan, sizes, lag):
        pieces = len(sizes)

        def call(*operands):
            return pl.pallas_call(
                functools.partial(helped_kernel, frames, parts, heads, columns, plan, sizes, lag),
                scratch_shapes=[
                    vmem((frames, 3, parts, rows, width), jnp.bfloat16),
                    vmem((2, heads, parts, rows, HEAD_DIM), jnp.bfloat16),
                    vmem((2, heads, parts, 8, rows), jnp.float32),
                    vmem((2, heads, parts, rows, HEAD_DIM), jnp.bfloat16),
                    vmem((2, heads, parts, 8, rows), jnp.float32),
                    vmem((heads, parts, rows, HEAD_DIM), jnp.bfloat16),
                    vmem((heads, parts, 8, rows), jnp.float32),
                    vmem((heads, parts, rows, HEAD_DIM), jnp.bfloat16),
                    vmem((heads, parts, 8, rows), jnp.float32),
                    vmem((parts, rows, width), jnp.bfloat16),
                    vmem((tokens, tokens), jnp.float32),
                    vmem((heads, 1, tokens), jnp.float32),
                    vmem((heads, 1, tokens), jnp.float32),
                    vmem((heads, HEAD_DIM, tokens), jnp.float32),
                    dma((3,)),
                    dma((3, others, pieces)),
                    dma((3, others, pieces)),
                    dma((2, 3, pieces)),
                    dma((2, 3, pieces)),
                    dma((2, parts, pieces)),
                    dma((2, parts, pieces)),
                    dma((2, 2, pieces)),
                    dma((2, 2, pieces)),
                    dma((2, heads, parts)),
                    dma((2, heads, parts)),
                    dma((2, heads, parts)),
                    dma((2, heads, parts)),
                    dma((2, heads, others)),
                    dma((2, heads, others)),
                    dma((others, heads)),
                    dma((others, heads)),
                ],
                in_specs=[any_spec] * 3 + [scalar_spec] * 2,
                compiler_params=pltpu.CompilerParams(
                    collective_id=collective_id, has_side_effects=True
                ),
                name=f"helped{collective_id}",
                **common,
            )(*operands)

        return call

    if far == 2:
        index, *chosen = pl.pallas_call(
            functools.partial(choose_kernel, frames),
            out_shape=[
                pltpu.SMEM((1,), jnp.int32),
                pltpu.SMEM(flags.shape, jnp.int32),
                pltpu.SMEM(widths.shape, jnp.int32),
            ],
            in_specs=[scalar_spec] * 2,
            out_specs=[scalar_spec] * 3,
            name="choose",
        )(flags, widths)
        inner = [(side, at) for side in (LEFT, RIGHT) for at in range(1, frames - 1)]
        far_left, far_right = (LEFT, frames - 2), (RIGHT, 1)
        front = min(1, heads - 1)
        back = max(heads - 2, 0)
        mixed = [n for n in [2] * (back // 2) + [back % 2] + [1] * (heads - back) if n]
        whole = {key: back if key in (far_left, far_right) else 0 for key in inner}
        branches = [helped(0, whole, mixed, heads)] + [
            helped(n, {key: None if key == gone else front for key in inner}, [1] * heads, lag)
            for n, gone, lag in ((1, far_left, 2), (2, far_right, 3))
        ]
        out = lax.switch(index[0], branches, *flat, *chosen)
    else:
        out = full(*flat, flags, widths)
    return out.reshape(shape)


def solution(mesh):
    spec = P(("group", "frame"), "space", None, "head")
    return jax.shard_map(
        functools.partial(shards, mesh.shape["frame"], mesh.shape["space"]),
        mesh=mesh,
        in_specs=(spec, spec, spec, P(), P()),
        out_specs=spec,
        check_vma=False,
    )
```

```python
import functools
import math

import jax
import jax.numpy as jnp
from jax import lax
from jax.experimental import pallas as pl
from jax.experimental.pallas import tpu as pltpu
from jax.sharding import PartitionSpec as P

HEAD_DIM = 128
NEG_FILL = -1e30
SCALE = math.log2(math.e) / HEAD_DIM**0.5
MESH = pl.DeviceIdType.MESH
LEFT, RIGHT = 0, 1


def kernel(
    frames,
    parts,
    heads,
    columns,
    q_ref,
    k_ref,
    v_ref,
    flags_in,
    widths_in,
    out_ref,
    kv,
    qb,
    ob,
    dist,
    wb,
    top,
    total,
    acc,
    local_sem,
    x_send,
    x_recv,
    z_send,
    z_recv,
    f_send,
    f_recv,
    o_send,
    o_recv,
    flags_ref,
    widths_ref,
    table_sem,
):
    frame = lax.axis_index("frame")
    part = lax.axis_index("space")
    rows = q_ref.shape[0]
    tokens = parts * rows
    width = heads * HEAD_DIM
    far = frames - 2
    inputs = (k_ref, v_ref, q_ref)

    def lane(head):
        return pl.ds(pl.multiple_of(head * HEAD_DIM, HEAD_DIM), HEAD_DIM)

    def span(p):
        return pl.ds(pl.multiple_of(p * width, HEAD_DIM), width)

    def peer(j):
        return lax.rem(part + j, parts)

    def home(i):
        return qb.at[part] if i == 2 else kv.at[frame, i, part]

    barrier = pltpu.get_barrier_semaphore()
    for j in range(1, parts):
        pl.semaphore_signal(barrier, inc=1, device_id={"space": peer(j)}, device_id_type=MESH)

    @pl.when(frame > 0)
    def _():
        pl.semaphore_signal(barrier, inc=1, device_id={"frame": frame - 1}, device_id_type=MESH)

    @pl.when(frame < frames - 1)
    def _():
        pl.semaphore_signal(barrier, inc=1, device_id={"frame": frame + 1}, device_id_type=MESH)

    def local_copy(i):
        return pltpu.make_async_copy(inputs[i].at[:, span(part)], home(i), local_sem.at[i])

    def exchange(j, i):
        return pltpu.make_async_remote_copy(
            src_ref=inputs[i].at[:, span(peer(j))],
            dst_ref=home(i),
            send_sem=x_send.at[i, j - 1],
            recv_sem=x_recv.at[i, j - 1],
            device_id={"space": peer(j)},
            device_id_type=MESH,
        )

    def o_exchange(h, j):
        return pltpu.make_async_remote_copy(
            src_ref=ob.at[peer(j), :, lane(h)],
            dst_ref=out_ref.at[:, lane(part * heads + h)],
            send_sem=o_send.at[j - 1, h],
            recv_sem=o_recv.at[j - 1, h],
            device_id={"space": peer(j)},
            device_id_type=MESH,
        )

    def towards(side):
        return 1 if side == RIGHT else -1

    def hop(side, step, i, p, src=None, back=False):
        ahead = towards(side)
        owner = frame - ahead * (step if back else step - 1)
        block = kv.at[owner, i, p]
        return pltpu.make_async_remote_copy(
            src_ref=block if src is None else src,
            dst_ref=block,
            send_sem=z_send.at[side, step - 1, i, p],
            recv_sem=z_recv.at[side, step - 1, i, p],
            device_id={"frame": frame - ahead if back else frame + ahead},
            device_id_type=MESH,
        )

    def fine(side, h, back=False):
        ahead = towards(side)
        owner = frame - ahead * (far if back else far - 1)
        block = kv.at[owner, 1, :, :, lane(h)]
        return pltpu.make_async_remote_copy(
            src_ref=block,
            dst_ref=block,
            send_sem=f_send.at[side, h],
            recv_sem=f_recv.at[side, h],
            device_id={"frame": frame - ahead if back else frame + ahead},
            device_id_type=MESH,
        )

    def can_send(side, step):
        if side == RIGHT:
            return (frame < frames - 1) & (frame - (step - 1) >= 0)
        return (frame > 0) & (frame + (step - 1) <= frames - 1)

    def gets(side, step):
        if side == RIGHT:
            return frame - step >= 0
        return frame + step <= frames - 1

    def source(side, step):
        return frame - step if side == RIGHT else frame + step

    def each_head(body):
        @pl.loop(0, heads)
        def _(h):
            body(h)

    pl.semaphore_wait(
        barrier,
        parts - 1 + jnp.where(frame > 0, 1, 0) + jnp.where(frame < frames - 1, 1, 0),
    )

    for i in (0, 1):
        for j in range(1, parts):
            exchange(j, i).start()
        for side in (LEFT, RIGHT):

            @pl.when(can_send(side, 1))
            def _():
                hop(side, 1, i, part, inputs[i].at[:, span(part)]).start()

    tables = (
        pltpu.make_async_copy(flags_in, flags_ref, table_sem.at[0]),
        pltpu.make_async_copy(widths_in, widths_ref, table_sem.at[1]),
    )
    for copy in tables:
        copy.start()
    for i in range(3):
        local_copy(i).start()
    for j in range(1, parts):
        exchange(j, 2).start()

    def row_of(axis):
        at = lax.broadcasted_iota(jnp.int32, (tokens, tokens), axis).astype(jnp.float32)
        return jnp.floor((at + 0.5) * (1.0 / columns))

    dist[...] = jnp.abs(row_of(0) - row_of(1))
    top[...] = jnp.full(top.shape, NEG_FILL, jnp.float32)
    total[...] = jnp.zeros(total.shape, jnp.float32)
    acc[...] = jnp.zeros(acc.shape, jnp.float32)

    def await_piece(side, step, i, p):
        @pl.when(gets(side, step))
        def _():
            hop(side, step, i, p, back=True).wait_recv()

    def relay_piece(side, step, i, p):
        @pl.when(gets(side, step) & can_send(side, step + 1))
        def _():
            hop(side, step + 1, i, p).start()

    def relay_fine(step):
        for side in (LEFT, RIGHT):

            @pl.when(gets(side, step) & can_send(side, step + 1))
            def _():
                each_head(lambda h: fine(side, h).start())

    def pass_piece(i):
        for j in range(1, parts):
            p = lax.rem(part - j + parts, parts)
            exchange(j, i).wait_recv()
            for side in (LEFT, RIGHT):

                @pl.when(can_send(side, 1))
                def _():
                    hop(side, 1, i, p).start()

    def take(step, i, p):
        for side in (LEFT, RIGHT):
            await_piece(side, step, i, p)
            if far > 1:
                relay_piece(side, step, i, p)

    pass_piece(0)
    take(1, 0, part)
    pass_piece(1)
    for copy in tables:
        copy.wait()

    def masked(h, g):
        gap = jnp.abs(frame - g)
        reach = jnp.where(flags_ref[frame, g] > 0, widths_ref[gap], -1).astype(jnp.float32)
        keys = kv[g, 0, :, :, lane(h)].reshape(tokens, HEAD_DIM)
        queries = qb[:, :, lane(h)].reshape(tokens, HEAD_DIM)
        scores = lax.dot_general(
            keys, queries, (((1,), (1,)), ((), ())), preferred_element_type=jnp.float32
        )
        scores = jnp.where(dist[...] <= reach, scores, NEG_FILL)
        old_top = top[h]
        new_top = jnp.maximum(old_top, jnp.max(scores, axis=0, keepdims=True))
        weights = jnp.exp2((scores - new_top) * SCALE)
        keep = jnp.exp2((old_top - new_top) * SCALE)
        top[h] = new_top
        total[h] = total[h] * keep + jnp.sum(weights, axis=0, keepdims=True)
        return weights.astype(jnp.bfloat16), keep

    def mixed(weights, h, g):
        vals = kv[g, 1, :, :, lane(h)].reshape(tokens, HEAD_DIM)
        return lax.dot_general(
            vals, weights, (((0,), (0,)), ((), ())), preferred_element_type=jnp.float32
        )

    def update(h, g):
        weights, keep = masked(h, g)
        acc[h] = acc[h] * keep + mixed(weights, h, g)

    def blend(step):
        def body(h):
            for side in (LEFT, RIGHT):

                @pl.when(gets(side, step))
                def _():
                    update(h, source(side, step))

        each_head(body)

    for j in range(1, parts):
        take(1, 0, peer(j))
    for i in range(3):
        local_copy(i).wait()
    for j in range(1, parts):
        exchange(j, 2).wait_recv()
    each_head(lambda h: update(h, frame))

    def take_values(step):
        for p in range(parts):
            for side in (LEFT, RIGHT):
                await_piece(side, step, 1, p)
                if far > 2:

                    @pl.when(step + 1 < far)
                    def _():
                        relay_piece(side, step, 1, p)

        if far > 1:
            if far == 2:
                relay_fine(step)
            else:

                @pl.when(step + 1 == far)
                def _():
                    relay_fine(step)

    take_values(1)
    blend(1)

    if far > 2:

        @pl.loop(2, far)
        def _(step):
            for p in range(parts):
                take(step, 0, p)
            take_values(step)
            blend(step)

    if far > 1:
        for p in range(parts):
            for side in (LEFT, RIGHT):
                await_piece(side, far, 0, p)

    def last(h):
        if far > 1:
            for side in (LEFT, RIGHT):

                @pl.when(gets(side, far))
                def _():
                    weights, keep = masked(h, source(side, far))
                    wb[side] = weights
                    acc[h] = acc[h] * keep

        if far > 1:
            for side in (LEFT, RIGHT):

                @pl.when(gets(side, far))
                def _():
                    fine(side, h, back=True).wait_recv()
                    acc[h] = acc[h] + mixed(wb[side], h, source(side, far))

        result = jnp.transpose(acc[h] * (1.0 / total[h])).astype(jnp.bfloat16)
        ob[:, :, lane(h)] = result.reshape(parts, rows, HEAD_DIM)
        for j in range(1, parts):
            o_exchange(h, j).start()
        out_ref[:, lane(part * heads + h)] = ob[part, :, lane(h)]

    each_head(last)

    def close_head(h):
        for j in range(1, parts):
            o_exchange(h, j).wait()
        if far > 1:
            for side in (LEFT, RIGHT):

                @pl.when(can_send(side, far))
                def _():
                    fine(side, h).wait_send()

    for i in range(3):
        for j in range(1, parts):
            exchange(j, i).wait_send()

    @pl.loop(1, far + 1)
    def _(step):
        for side in (LEFT, RIGHT):

            @pl.when(can_send(side, step))
            def _():
                for p in range(parts):
                    hop(side, step, 0, p).wait_send()

                    @pl.when((step < far) | (step == 1))
                    def _():
                        hop(side, step, 1, p).wait_send()

    each_head(close_head)


def head_groups(sizes):
    edges = [sum(sizes[:n]) for n in range(len(sizes) + 1)]
    return list(zip(edges[:-1], edges[1:]))


def helped_kernel(
    frames,
    parts,
    heads,
    columns,
    plan,
    sizes,
    lag,
    q_ref,
    k_ref,
    v_ref,
    flags_ref,
    widths_ref,
    out_ref,
    kvq,
    given,
    given_stat,
    got,
    got_stat,
    mine,
    mine_stat,
    held,
    held_stat,
    ob,
    dist,
    top,
    total,
    acc,
    local_sem,
    x_send,
    x_recv,
    n_send,
    n_recv,
    p_send,
    p_recv,
    r_send,
    r_recv,
    a_send,
    a_recv,
    s_send,
    s_recv,
    m_send,
    m_recv,
    o_send,
    o_recv,
):
    frame = lax.axis_index("frame")
    part = lax.axis_index("space")
    rows = q_ref.shape[0]
    tokens = parts * rows
    inputs = (k_ref, v_ref, q_ref)
    groups = head_groups(sizes)

    def lane(head, count=1):
        return pl.ds(pl.multiple_of(head * HEAD_DIM, HEAD_DIM), count * HEAD_DIM)

    def piece(gi, p=None):
        low, high = groups[gi]
        return lane(low if p is None else p * heads + low, high - low)

    def peer(j):
        return lax.rem(part + j, parts)

    def giver(j):
        return lax.rem(part - j + parts, parts)

    def ahead(side):
        return 1 if side == RIGHT else -1

    def where(helper, side, test):
        found = None
        for at in range(1, frames - 1):
            kept = plan[side, at]
            term = None if kept is None else test(kept)
            if term is None or term is False:
                continue
            term = (helper == at) if term is True else (helper == at) & term
            found = term if found is None else found | term
        return found

    def helped(helper, side, h):
        return where(helper, side, lambda r: False if r == heads else (h >= r if r > 0 else True))

    def relayed(helper, side, h):
        return where(helper, side, lambda r: False if r == 0 else (h < r if r < heads else True))

    def when(condition, body):
        if condition is not None:
            pl.when(condition)(body)

    def has(side):
        return frame < frames - 1 if side == RIGHT else frame > 0

    def near(side):
        return frame > 0 if side == RIGHT else frame < frames - 1

    barrier = pltpu.get_barrier_semaphore()
    for j in range(1, parts):
        pl.semaphore_signal(barrier, inc=1, device_id={"space": peer(j)}, device_id_type=MESH)
    for side in (LEFT, RIGHT):

        @pl.when(has(side))
        def _():
            for p in range(parts):
                pl.semaphore_signal(
                    barrier,
                    inc=1,
                    device_id={"frame": frame + ahead(side), "space": p},
                    device_id_type=MESH,
                )

    pl.semaphore_wait(
        barrier,
        parts - 1 + jnp.where(frame > 0, parts, 0) + jnp.where(frame < frames - 1, parts, 0),
    )

    def local_copy(i):
        return pltpu.make_async_copy(
            inputs[i].at[:, lane(part * heads, heads)], kvq.at[frame, i, part], local_sem.at[i]
        )

    def exchange(j, i, gi):
        return pltpu.make_async_remote_copy(
            src_ref=inputs[i].at[:, piece(gi, peer(j))],
            dst_ref=kvq.at[frame, i, part, :, piece(gi)],
            send_sem=x_send.at[i, j - 1, gi],
            recv_sem=x_recv.at[i, j - 1, gi],
            device_id={"space": peer(j)},
            device_id_type=MESH,
        )

    def own_hop(side, i, gi, back=False):
        owner = frame - ahead(side) if back else frame
        return pltpu.make_async_remote_copy(
            src_ref=inputs[i].at[:, piece(gi, part)],
            dst_ref=kvq.at[owner, i, part, :, piece(gi)],
            send_sem=n_send.at[side, i, gi],
            recv_sem=n_recv.at[side, i, gi],
            device_id={"frame": owner if back else frame + ahead(side)},
            device_id_type=MESH,
        )

    def slab_hop(side, p, slot, gi, query, back=False):
        owner = frame - ahead(side) if back else frame
        slab = kvq.at[owner, pl.ds(0, 3 if query else 2), p, :, piece(gi)]
        return pltpu.make_async_remote_copy(
            src_ref=slab,
            dst_ref=slab,
            send_sem=p_send.at[side, slot, gi],
            recv_sem=p_recv.at[side, slot, gi],
            device_id={"frame": owner if back else frame + ahead(side)},
            device_id_type=MESH,
        )

    def relay(side, i, gi, back=False):
        owner = frame - (2 if back else 1) * ahead(side)
        slab = kvq.at[owner, pl.ds(0, 2) if i is None else pl.ds(i, 1), :, :, piece(gi)]
        return pltpu.make_async_remote_copy(
            src_ref=slab,
            dst_ref=slab,
            send_sem=r_send.at[side, i or 0, gi],
            recv_sem=r_recv.at[side, i or 0, gi],
            device_id={"frame": frame - ahead(side) if back else frame + ahead(side)},
            device_id_type=MESH,
        )

    def answer(side, h, p, back=False):
        to = frame - ahead(side) if back else frame + ahead(side)
        slot = p if back else part
        return tuple(
            pltpu.make_async_remote_copy(
                src_ref=src.at[side, h, p],
                dst_ref=dst.at[side, h, slot],
                send_sem=send.at[side, h, p],
                recv_sem=recv.at[side, h, slot],
                device_id={"frame": to, "space": p},
                device_id_type=MESH,
            )
            for src, dst, send, recv in (
                (given, got, a_send, a_recv),
                (given_stat, got_stat, s_send, s_recv),
            )
        )

    def share(h, j, back=False):
        slot = giver(j) if back else part
        to = peer(j)
        return tuple(
            pltpu.make_async_remote_copy(
                src_ref=src.at[h, to],
                dst_ref=dst.at[h, slot],
                send_sem=m_send.at[n, h, j - 1],
                recv_sem=m_recv.at[n, h, j - 1],
                device_id={"space": to},
                device_id_type=MESH,
            )
            for n, (src, dst) in enumerate(((mine, held), (mine_stat, held_stat)))
        )

    def o_exchange(h, j):
        return pltpu.make_async_remote_copy(
            src_ref=ob.at[peer(j), :, lane(h)],
            dst_ref=out_ref.at[:, lane(part * heads + h)],
            send_sem=o_send.at[j - 1, h],
            recv_sem=o_recv.at[j - 1, h],
            device_id={"space": peer(j)},
            device_id_type=MESH,
        )

    def opposite(side):
        return LEFT if side == RIGHT else RIGHT

    def sends_query(side, gi):
        return helped(frame + ahead(side), opposite(side), groups[gi][0])

    def takes_query(side, gi):
        return helped(frame, opposite(side), groups[gi][0])

    def direct(gi):
        return gi in (0, len(groups) - 1)

    def each_side(side, gi, query, plain, asked):
        if query is None:
            pl.when(plain)(lambda: asked(False))
        else:
            pl.when(query)(lambda: asked(True))
            pl.when(plain & jnp.logical_not(query))(lambda: asked(False))

    def each_own(gi, act):
        for side in (LEFT, RIGHT):
            query = sends_query(side, gi)
            if direct(gi):
                for i in (0, 1, 2):
                    when(query if i == 2 else has(side), lambda: act(own_hop(side, i, gi)))
            else:
                each_side(
                    side, gi, query, has(side), lambda q: act(slab_hop(side, part, 0, gi, q))
                )

    def each_pass(gi, act):
        for j in range(1, parts):
            for side in (LEFT, RIGHT):
                each_side(
                    side,
                    gi,
                    sends_query(side, gi),
                    has(side),
                    lambda q: act(slab_hop(side, giver(j), j, gi, q)),
                )

    def relay_steps(gi):
        return (0, 1) if gi == len(groups) - 1 else (None,)

    def each_relay(gi, act):
        for side in (LEFT, RIGHT):
            for i in relay_steps(gi):
                when(relayed(frame, side, groups[gi][0]), lambda: act(relay(side, i, gi)))

    def begin(copy):
        copy.start()

    def drain(copy):
        copy.wait_send()

    def forward(gi):
        for i in range(3):
            for j in range(1, parts):
                exchange(j, i, gi).wait_recv()
            if i == 0:
                continue
            for j in range(1, parts):
                for side in (LEFT, RIGHT):
                    query = sends_query(side, gi)
                    ready = query
                    if i == 1:
                        ready = has(side)
                        if query is not None:
                            ready = ready & jnp.logical_not(query)
                    when(ready, lambda: slab_hop(side, giver(j), j, gi, i == 2).start())

    order = list(range(len(groups)))
    for j in range(1, parts):
        for i in range(3):
            exchange(j, i, 0).start()
    each_own(0, begin)
    if len(groups) > 1:
        each_own(order[-1], begin)
    for gi in order[1:]:
        for j in range(1, parts):
            for i in range(3):
                exchange(j, i, gi).start()
    for i in range(3):
        local_copy(i).start()

    def row_of(axis):
        at = lax.broadcasted_iota(jnp.int32, (tokens, tokens), axis).astype(jnp.float32)
        return jnp.floor((at + 0.5) * (1.0 / columns))

    dist[...] = jnp.abs(row_of(0) - row_of(1))
    top[...] = jnp.full(top.shape, NEG_FILL, jnp.float32)
    total[...] = jnp.zeros(total.shape, jnp.float32)
    acc[...] = jnp.zeros(acc.shape, jnp.float32)
    for i in range(3):
        local_copy(i).wait()

    for gi in order[:-1]:
        forward(gi)
        if gi + 1 < len(groups) - 1:
            each_own(gi + 1, begin)
    forward(order[-1])

    def await_group(gi):
        for side in (LEFT, RIGHT):
            query = takes_query(side, gi)
            if direct(gi):
                for i in (0, 1, 2):
                    when(
                        query if i == 2 else near(side),
                        lambda: own_hop(side, i, gi, back=True).wait_recv(),
                    )
            for slot in range(1 if direct(gi) else 0, parts):
                p = giver(slot) if slot else part
                each_side(
                    side,
                    gi,
                    query,
                    near(side),
                    lambda q: slab_hop(side, p, slot, gi, q, back=True).wait_recv(),
                )
        each_relay(gi, begin)

    def whole(f, i, h):
        return kvq[f, i, :, :, lane(h)].reshape(tokens, HEAD_DIM)

    def scores_of(h, f, g):
        gap = jnp.abs(f - g)
        reach = jnp.where(flags_ref[f, g] > 0, widths_ref[gap], -1).astype(jnp.float32)
        scores = lax.dot_general(
            whole(g, 0, h),
            whole(f, 2, h),
            (((1,), (1,)), ((), ())),
            preferred_element_type=jnp.float32,
        )
        return jnp.where(dist[...] <= reach, scores, NEG_FILL)

    def mixed(weights, h, g):
        return lax.dot_general(
            whole(g, 1, h),
            weights.astype(jnp.bfloat16),
            (((0,), (0,)), ((), ())),
            preferred_element_type=jnp.float32,
        )

    def update(h, g, between=None):
        scores = scores_of(h, frame, g)
        old_top = top[h]
        new_top = jnp.maximum(old_top, jnp.max(scores, axis=0, keepdims=True))
        weights = jnp.exp2((scores - new_top) * SCALE)
        keep = jnp.exp2((old_top - new_top) * SCALE)
        top[h] = new_top
        total[h] = total[h] * keep + jnp.sum(weights, axis=0, keepdims=True)
        if between is not None:
            between()
        acc[h] = acc[h] * keep + mixed(weights, h, g)

    def split(values, stats, result, peak, mass):
        turned = jnp.transpose(result).astype(jnp.bfloat16)
        for p in range(parts):
            cut = slice(p * rows, (p + 1) * rows)
            values[p] = turned[cut]
            stats[p, 0:1] = peak[:, cut]
            stats[p, 1:2] = mass[:, cut]

    def help_with(side, h):
        f, g = frame + ahead(side), frame - ahead(side)
        scores = scores_of(h, f, g)
        peak = jnp.max(scores, axis=0, keepdims=True)
        weights = jnp.exp2((scores - peak) * SCALE)
        split(
            given.at[side, h],
            given_stat.at[side, h],
            mixed(weights, h, g),
            peak,
            jnp.sum(weights, axis=0, keepdims=True),
        )
        for p in range(parts):
            for copy in answer(side, h, p):
                copy.start()

    def compute(h):
        for gi, (low, _high) in enumerate(groups):

            @pl.when(h == low)
            def _():
                await_group(gi)

        for side in (LEFT, RIGHT):
            when(helped(frame, side, h), lambda: help_with(side, h))

        update(h, frame)
        for side in (LEFT, RIGHT):

            @pl.when(near(side))
            def _():
                update(h, frame - ahead(side))

        def share_all():
            split(mine.at[h], mine_stat.at[h], acc[h], top[h], total[h])
            for j in range(1, parts):
                for copy in share(h, j):
                    copy.start()

        for side in (LEFT, RIGHT):
            when(helped(frame - ahead(side), side, h), share_all)

    def await_relay(side, i, h):
        for gi, (low, _high) in enumerate(groups):
            steps = relay_steps(gi)
            if relayed(frame - ahead(side), side, low) is None or (i and i not in steps):
                continue

            @pl.when(h == low)
            def _():
                relay(side, i if i in steps else None, gi, back=True).wait_recv()

    def take_relay(side, h):
        await_relay(side, 0, h)
        update(h, frame - 2 * ahead(side), lambda: await_relay(side, 1, h))

    def merge(h, p, values, stats, far_values, far_stats):
        peak, far_peak = stats[0:1], far_stats[0:1]
        new_top = jnp.maximum(peak, far_peak)
        keep = jnp.exp2((peak - new_top) * SCALE)
        add = jnp.exp2((far_peak - new_top) * SCALE)
        mass = 1.0 / (stats[1:2] * keep + far_stats[1:2] * add)
        share_of = jnp.concatenate([keep * mass, add * mass] * 4, axis=0)
        column = jnp.transpose(share_of)
        result = values[...].astype(jnp.float32) * column[:, 0:1]
        result = result + far_values[...].astype(jnp.float32) * column[:, 1:2]
        out_ref[:, lane(p * heads + h)] = result.astype(jnp.bfloat16)

    def take_answer(side, h):
        for j in range(parts):
            p = giver(j) if j else part
            if j:
                for copy in share(h, j, back=True):
                    copy.wait_recv()
            for copy in answer(side, h, p, back=True):
                copy.wait_recv()
            kept, kept_stat = (held, held_stat) if j else (mine, mine_stat)
            merge(h, p, kept.at[h, p], kept_stat.at[h, p], got.at[side, h, p], got_stat.at[side, h, p])

    def elsewhere(h):
        answered = None
        for side in (LEFT, RIGHT):
            term = helped(frame - ahead(side), side, h)
            if term is not None:
                answered = term if answered is None else answered | term
        return answered

    def unless(condition, body):
        if condition is None:
            body()
        else:
            pl.when(jnp.logical_not(condition))(body)

    def finish(h):
        for side in (LEFT, RIGHT):
            helper = frame - ahead(side)
            when(relayed(helper, side, h), lambda: take_relay(side, h))
            when(helped(helper, side, h), lambda: take_answer(side, h))

        def write():
            result = jnp.transpose(acc[h] * (1.0 / total[h])).astype(jnp.bfloat16)
            ob[:, :, lane(h)] = result.reshape(parts, rows, HEAD_DIM)
            for j in range(1, parts):
                o_exchange(h, j).start()
            out_ref[:, lane(part * heads + h)] = ob[part, :, lane(h)]

        unless(elsewhere(h), write)

    @pl.loop(0, heads + lag)
    def _(step):
        @pl.when(step < heads)
        def _():
            compute(step)

        @pl.when(step >= lag)
        def _():
            finish(step - lag)

    for gi in order:
        for j in range(1, parts):
            for i in range(3):
                exchange(j, i, gi).wait_send()
        each_own(gi, drain)
        each_pass(gi, drain)
        each_relay(gi, drain)

    @pl.loop(0, heads)
    def _(h):
        for side in (LEFT, RIGHT):

            def drained():
                for p in range(parts):
                    for copy in answer(side, h, p):
                        copy.wait_send()

            def shared():
                for j in range(1, parts):
                    for copy in share(h, j):
                        copy.wait_send()

            when(helped(frame, side, h), drained)
            when(helped(frame - ahead(side), side, h), shared)

        def written():
            for j in range(1, parts):
                o_exchange(h, j).wait()

        unless(elsewhere(h), written)


def choose_kernel(frames, flags_in, widths_in, index_ref, flags_ref, widths_ref):
    right = flags_in[frames - 2, 0] > 0
    left = flags_in[1, frames - 1] > 0
    index_ref[0] = jnp.where(left, jnp.where(right, 0, 2), 1)
    for f in range(frames):
        widths_ref[f] = widths_in[f]
        for g in range(frames):
            flags_ref[f, g] = flags_in[f, g]


def shards(frames, parts, queries, keys, values, flags, widths):
    shape = queries.shape
    columns, features = shape[2], shape[3]
    rows = shape[1] * columns
    heads = features // HEAD_DIM // parts
    tokens = rows * parts
    far = frames - 2
    flat = [a.reshape(rows, features) for a in (queries, keys, values)]
    any_spec = pl.BlockSpec(memory_space=pl.ANY)
    others = max(parts - 1, 1)
    dma = pltpu.SemaphoreType.DMA
    vmem = pltpu.VMEM
    width = heads * HEAD_DIM
    tables = [pltpu.SMEM(flags.shape, jnp.int32), pltpu.SMEM(widths.shape, jnp.int32), dma((2,))]
    scalar_spec = pl.BlockSpec(memory_space=pltpu.SMEM)
    common = dict(
        out_shape=vmem((rows, features), jnp.bfloat16),
        out_specs=pl.BlockSpec(memory_space=vmem),
    )

    def full(*operands):
        return pl.pallas_call(
            functools.partial(kernel, frames, parts, heads, columns),
            scratch_shapes=[
                vmem((frames, 2, parts, rows, width), jnp.bfloat16),
                vmem((parts, rows, width), jnp.bfloat16),
                vmem((parts, rows, width), jnp.bfloat16),
                vmem((tokens, tokens), jnp.float32),
                vmem((2, tokens, tokens), jnp.bfloat16),
                vmem((heads, 1, tokens), jnp.float32),
                vmem((heads, 1, tokens), jnp.float32),
                vmem((heads, HEAD_DIM, tokens), jnp.float32),
                dma((3,)),
                dma((3, others)),
                dma((3, others)),
                dma((2, far, 2, parts)),
                dma((2, far, 2, parts)),
                dma((2, heads)),
                dma((2, heads)),
                dma((others, heads)),
                dma((others, heads)),
            ]
            + tables,
            compiler_params=pltpu.CompilerParams(collective_id=0, has_side_effects=True),
            in_specs=[any_spec] * 5,
            name="full",
            **common,
        )(*operands)

    def helped(collective_id, plan, sizes, lag):
        pieces = len(sizes)

        def call(*operands):
            return pl.pallas_call(
                functools.partial(helped_kernel, frames, parts, heads, columns, plan, sizes, lag),
                scratch_shapes=[
                    vmem((frames, 3, parts, rows, width), jnp.bfloat16),
                    vmem((2, heads, parts, rows, HEAD_DIM), jnp.bfloat16),
                    vmem((2, heads, parts, 8, rows), jnp.float32),
                    vmem((2, heads, parts, rows, HEAD_DIM), jnp.bfloat16),
                    vmem((2, heads, parts, 8, rows), jnp.float32),
                    vmem((heads, parts, rows, HEAD_DIM), jnp.bfloat16),
                    vmem((heads, parts, 8, rows), jnp.float32),
                    vmem((heads, parts, rows, HEAD_DIM), jnp.bfloat16),
                    vmem((heads, parts, 8, rows), jnp.float32),
                    vmem((parts, rows, width), jnp.bfloat16),
                    vmem((tokens, tokens), jnp.float32),
                    vmem((heads, 1, tokens), jnp.float32),
                    vmem((heads, 1, tokens), jnp.float32),
                    vmem((heads, HEAD_DIM, tokens), jnp.float32),
                    dma((3,)),
                    dma((3, others, pieces)),
                    dma((3, others, pieces)),
                    dma((2, 3, pieces)),
                    dma((2, 3, pieces)),
                    dma((2, parts, pieces)),
                    dma((2, parts, pieces)),
                    dma((2, 2, pieces)),
                    dma((2, 2, pieces)),
                    dma((2, heads, parts)),
                    dma((2, heads, parts)),
                    dma((2, heads, parts)),
                    dma((2, heads, parts)),
                    dma((2, heads, others)),
                    dma((2, heads, others)),
                    dma((others, heads)),
                    dma((others, heads)),
                ],
                in_specs=[any_spec] * 3 + [scalar_spec] * 2,
                compiler_params=pltpu.CompilerParams(
                    collective_id=collective_id, has_side_effects=True
                ),
                name=f"helped{collective_id}",
                **common,
            )(*operands)

        return call

    if far == 2:
        index, *chosen = pl.pallas_call(
            functools.partial(choose_kernel, frames),
            out_shape=[
                pltpu.SMEM((1,), jnp.int32),
                pltpu.SMEM(flags.shape, jnp.int32),
                pltpu.SMEM(widths.shape, jnp.int32),
            ],
            in_specs=[scalar_spec] * 2,
            out_specs=[scalar_spec] * 3,
            name="choose",
        )(flags, widths)
        inner = [(side, at) for side in (LEFT, RIGHT) for at in range(1, frames - 1)]
        far_left, far_right = (LEFT, frames - 2), (RIGHT, 1)
        front = min(1, heads - 1)
        back = max(heads - 2, 0)
        mixed = [n for n in [2] * (back // 2) + [back % 2] + [1] * (heads - back) if n]
        paired = [1, 1, 2] + [1] * (heads - 4) if heads > 4 else [1] * heads
        whole = {key: back if key in (far_left, far_right) else 0 for key in inner}
        branches = [helped(0, whole, mixed, heads)] + [
            helped(n, {key: None if key == gone else front for key in inner}, paired, lag)
            for n, gone, lag in ((1, far_left, 2), (2, far_right, 3))
        ]
        out = lax.switch(index[0], branches, *flat, *chosen)
    else:
        out = full(*flat, flags, widths)
    return out.reshape(shape)


def solution(mesh):
    spec = P(("group", "frame"), "space", None, "head")
    return jax.shard_map(
        functools.partial(shards, mesh.shape["frame"], mesh.shape["space"]),
        mesh=mesh,
        in_specs=(spec, spec, spec, P(), P()),
        out_specs=spec,
        check_vma=False,
    )
```
